256 devices in a mesh: wide: 64 (over z, x_hi, y), narrow: 4 (over x_lo, core).
Axes of the slice: x: 4 (x_hi: 2, x_lo: 2; x = x_hi * 2 + x_lo), y: 4, z: 8, core: 2. Of those that a mesh axis runs over, the one named last changes fastest.
Arguments:
- occupied: bfloat16 [512, 64, 4096], P('wide', 'narrow'), may hold values from -6 to 6
- empty: bfloat16 [1024, 64, 4096], P('wide', 'narrow'), may hold values from -6 to 6
- pair_occ: int32 [2048], P('wide'), may hold values from 0 to 7
- pair_emp: int32 [2048], P('wide'), may hold values from 0 to 15
- pair_level: int32 [2048], replicated, may hold values from 0 to 63
- denominators: float32 [64, 8], replicated, may hold values from 0.02 to 0.2
- trial: bfloat16 [131072, 512], P(('wide', 'narrow')), may hold values from -0.015625 to 0.015625
Outputs:
- response: bfloat16 [8, 131072, 512], P(None, ('wide', 'narrow'))
The draws below stay inside these ranges and needn't reach their ends.
Inputs may be any that keep to these rules, and one draw needn't show every extreme that they name: Pair p uses occupied band (p // 32) * 8 + pair_occ[p]. Pair p uses empty band (p // 32) * 16 + pair_emp[p].
All inputs are finite; a program needn't handle non-finite values.
Results may differ from the reference program's by a relative error of at most 0.012.
Values may be sent and summed in bfloat16 or wider, within the bound.
A program may use at most 128 MiB of HBM per device.

```python
import math
import jax
import jax.numpy as jnp
from jax import lax

GRID = 64
K = 512
NW = 8
NTAB = 64
OCC_DEV = 8
EMP_DEV = 16
P_DEV = 32
N_OCC = 512
N_EMP = 1024
PAIRS = 2048
COLS = 131072
N_WIDE = 64
N_NARROW = 4


def touch_ends(result, rng, least, largest):
    longest = result.shape.index(max(result.shape))
    spots = []
    for shift in (0, 1):
        where = [jax.random.randint(jax.random.fold_in(rng, axis), (), 0, length) for axis, length in enumerate(result.shape)]
        where[longest] = (where[longest] + shift) % result.shape[longest]
        spots.append(tuple(where))
    return result.at[spots[0]].set(least).at[spots[1]].set(largest)


def block_scale(stream_key, dims, shards, least, high):
    level = 1.0
    for axis_at, parts in shards:
        steps = jax.random.uniform(jax.random.fold_in(jax.random.fold_in(stream_key, 6), axis_at), (parts,), jnp.float32, least / len(shards), high / len(shards))
        level = level * jnp.repeat(jnp.exp(steps), dims[axis_at] // parts).reshape((-1,) + (1,) * (len(dims) - 1 - axis_at))
    return level


def normal_values(rng, shape, width, most, cuts=(), held_as=jnp.bfloat16):
    array = width * jax.random.normal(rng, shape, jnp.float32)
    if cuts:
        array = array * block_scale(rng, shape, cuts, -0.22, 0.18)
    return jnp.clip(array, -most, most).astype(held_as)


def setup_inputs(seed: int = 0) -> dict:
    key_list = jax.random.split(jax.random.key(seed), 8)
    return {
        "occupied": normal_values(key_list[0], (N_OCC, GRID, GRID * GRID), 1.0, 6.0, ((0, 64), (1, 4))),
        "empty": normal_values(key_list[1], (N_EMP, GRID, GRID * GRID), 1.0, 6.0, ((0, 64), (1, 4))),
        "pair_occ": touch_ends(jax.random.randint(key_list[2], (PAIRS,), 0, OCC_DEV), jax.random.fold_in(key_list[2], 1), 0, OCC_DEV - 1).astype(jnp.int32),
        "pair_emp": touch_ends(jax.random.randint(key_list[3], (PAIRS,), 0, EMP_DEV), jax.random.fold_in(key_list[3], 1), 0, EMP_DEV - 1).astype(jnp.int32),
        "pair_level": touch_ends(jax.random.randint(key_list[4], (PAIRS,), 0, NTAB), jax.random.fold_in(key_list[4], 1), 0, NTAB - 1).astype(jnp.int32),
        "denominators": jnp.clip(jnp.exp(jax.random.uniform(key_list[5], (NTAB, NW), jnp.float32, math.log(0.02), math.log(0.2))), 0.02, 0.2),
        "trial": normal_values(key_list[6], (COLS, K), COLS ** -0.5, 0.015625, ((0, 256),)),
    }


def tables(grid_size):
    positions = jnp.arange(grid_size, dtype=jnp.int32)
    half_range = jnp.arange(grid_size // 2, dtype=jnp.int32)
    scaling = 1.0 / math.sqrt(grid_size)
    step_angle = 2.0 * math.pi / grid_size
    z_angles = (positions[:, None] * half_range[None, :] % grid_size).astype(jnp.float32) * step_angle
    z_table = jnp.stack([jnp.cos(z_angles), -jnp.sin(z_angles)], -1).reshape(grid_size, grid_size) * scaling
    signed = jnp.where(half_range < grid_size // 4, half_range, half_range - grid_size // 2)
    y_angles = (signed[:, None] * positions[None, :] % grid_size).astype(jnp.float32) * step_angle
    y_table = jnp.stack([jnp.cos(y_angles), jnp.sin(y_angles)]) * scaling
    x_angles = (positions[:, None] * positions[None, :] % grid_size).astype(jnp.float32) * step_angle
    x_table = jnp.stack([jnp.cos(x_angles), jnp.sin(x_angles)]) * scaling
    return (z_table.astype(jnp.bfloat16), y_table.astype(jnp.bfloat16), x_table.astype(jnp.bfloat16))

def combine_parts(stacked):
    full_shape = stacked.shape[1:]
    halves = stacked.reshape(stacked.shape[:-1] + (stacked.shape[-1] // 2, 2))
    real_part = halves[0, ..., 0] + halves[1, ..., 1]
    imag_part = halves[0, ..., 1] - halves[1, ..., 0]
    return jnp.stack([real_part, imag_part], -1).reshape(full_shape)

def arrange(values, grid_size):
    values = values.reshape(grid_size, grid_size // 2, N_NARROW, grid_size // N_NARROW)
    values = jnp.transpose(values, (2, 0, 1, 3)).reshape(N_NARROW, N_WIDE, -1)
    return jnp.transpose(values, (1, 0, 2)).reshape(-1)

def coulomb_vector(grid_size):
    freq_x = jnp.arange(grid_size, dtype=jnp.int32)
    freq_x = jnp.where(freq_x < grid_size // 2, freq_x, freq_x - grid_size)
    freq_y = jnp.arange(grid_size // 2, dtype=jnp.int32)
    freq_y = jnp.where(freq_y < grid_size // 4, freq_y, freq_y - grid_size // 2)
    freq_z = jnp.arange(grid_size, dtype=jnp.int32) // 2
    squared = (freq_x[:, None, None] ** 2 + freq_y[None, :, None] ** 2 + freq_z[None, None, :] ** 2).astype(jnp.float32)
    quarter = float(grid_size // 4)
    return arrange(1.0 / jnp.sqrt(1.0 + squared / (quarter * quarter)), grid_size)

def pair_row(products, z_table, y_table, x_table):
    grid_size = products.shape[0]
    along_z = jnp.einsum('xyz,za->xya', products.astype(jnp.float32), z_table.astype(jnp.float32)).astype(jnp.bfloat16)
    along_y = combine_parts(jnp.einsum('sky,xyq->sxkq', y_table.astype(jnp.float32), along_z.astype(jnp.float32))).astype(jnp.bfloat16)
    along_x = combine_parts(jnp.einsum('skx,xyq->skyq', x_table.astype(jnp.float32), along_y.astype(jnp.float32))).astype(jnp.bfloat16)
    return arrange(along_x, grid_size)

def reference(occupied, empty, pair_occ, pair_emp, pair_level, denominators, trial):
    z_table, y_table, x_table = tables(GRID)
    pair_index = jnp.arange(pair_occ.shape[0], dtype=jnp.int32)
    occ_index = pair_index // P_DEV * OCC_DEV + pair_occ
    emp_index = pair_index // P_DEV * EMP_DEV + pair_emp

    def pair_wave(indices):
        products = (occupied[indices[0]].astype(jnp.float32) * empty[indices[1]].astype(jnp.float32)).astype(jnp.bfloat16)
        return pair_row(products.reshape(GRID, GRID, GRID), z_table, y_table, x_table)
    pair_waves = lax.map(pair_wave, jnp.stack([occ_index, emp_index], 1))
    coulomb = coulomb_vector(GRID)
    scaled = (coulomb[:, None] * trial.astype(jnp.float32)).astype(jnp.bfloat16)
    projections = jnp.dot(pair_waves, scaled, preferred_element_type=jnp.float32)
    weights = denominators[pair_level]
    weighted = (jnp.transpose(weights)[:, :, None] * projections[None]).astype(jnp.bfloat16)
    total_cols = pair_waves.shape[1]
    block_width = math.gcd(total_cols, 4096)
    weighted_wide = weighted.astype(jnp.float32)

    def column_block(block_index):
        pair_block = lax.dynamic_slice_in_dim(pair_waves, block_index * block_width, block_width, 1)
        product_sum = jnp.einsum('pc,wpk->wck', pair_block.astype(jnp.float32), weighted_wide)
        coulomb_block = lax.dynamic_slice_in_dim(coulomb, block_index * block_width, block_width, 0)
        return (product_sum * coulomb_block[None, :, None]).astype(jnp.bfloat16)
    blocks = lax.map(column_block, jnp.arange(total_cols // block_width, dtype=jnp.int32))
    return jnp.transpose(blocks, (1, 0, 2, 3)).reshape(NW, total_cols, trial.shape[1])
```

```python
import math

import jax
import jax.numpy as jnp
import ml_dtypes
import numpy as np
from jax import lax
from jax.experimental import pallas as pl
from jax.experimental.pallas import tpu as pltpu
from jax.sharding import PartitionSpec as P

GRID = 64
MESH = pl.DeviceIdType.MESH
F32, BF16 = jnp.float32, jnp.bfloat16
LIMIT = 60 * 1024 * 1024


def rounded(values):
    return values.astype(np.float32).astype(ml_dtypes.bfloat16).astype(np.float32)


def tables():
    at = np.arange(GRID)
    half = np.arange(GRID // 2)
    scaling = 1.0 / math.sqrt(GRID)
    step = 2.0 * math.pi / GRID
    z_angles = (at[:, None] * half[None, :] % GRID) * step
    z_real = rounded(scaling * np.cos(z_angles))
    z_imag = rounded(-scaling * np.sin(z_angles))
    signed = np.where(half < GRID // 4, half, half - GRID // 2)
    y_angles = (signed[:, None] * at[None, :] % GRID) * step
    y_cos = rounded(scaling * np.cos(y_angles))
    y_sin = rounded(scaling * np.sin(y_angles))
    x_angles = (at[:, None] * at[None, :] % GRID) * step
    x_cos = rounded(scaling * np.cos(x_angles))
    x_sin = rounded(scaling * np.sin(x_angles))
    zr = z_real.reshape(GRID, 4, 8).transpose(1, 0, 2)
    zi = z_imag.reshape(GRID, 4, 8).transpose(1, 0, 2)

    def spread(first, second):
        both = np.stack([first, second], 2)[:, :, :, None, :]
        return np.broadcast_to(both, (4, GRID, 2, 16, 8)).reshape(4, GRID, 256)

    z_first = spread(zr, zi)
    z_second = spread(zi, -zr)

    def widen(table):
        table = table[:, :32].reshape(16, 2, 32).transpose(1, 2, 0)
        return np.broadcast_to(table[:, :, None, :, None], (2, 32, 2, 16, 8)).reshape(2, 32, 256)

    x_table = np.block([[x_cos, x_sin], [-x_sin, x_cos]])
    perm = np.zeros((512, 512), np.float32)
    part, parity, j16, kz8 = np.meshgrid(np.arange(2), np.arange(2), np.arange(16), np.arange(8), indexing="ij")
    inner = np.arange(512)
    outer = ((2 * j16 + parity) * 16 + 2 * kz8 + part).reshape(-1)
    perm[outer, inner] = 1.0
    small = [z_first, z_second, widen(y_cos), widen(y_sin), x_table, perm]
    return [np.ascontiguousarray(t).astype(ml_dtypes.bfloat16) for t in small]


def plane_kernel(occ_at, emp_at, occ_ref, emp_ref, z_first, z_second, y_cos, y_sin, out_ref, x_scr, w_scr):
    @pl.loop(0, 32)
    def _(pair):
        product = occ_ref[occ_at[pair]].astype(F32) * emp_ref[emp_at[pair]].astype(F32)
        low, high = product[:, :2048], product[:, 2048:]
        rows = pl.ds(pl.multiple_of(pair * 16, 16), 16)
        x_scr[0, rows, :] = (low + high).astype(BF16)
        x_scr[1, rows, :] = (low - high).astype(BF16)

    for parity in range(2):
        for n in range(4):
            first = z_first[n].astype(F32)
            second = z_second[n].astype(F32)

            @pl.loop(0, 4)
            def _(group):
                cos8 = y_cos[parity, pl.ds(pl.multiple_of(group * 8, 8), 8), :].astype(F32)
                sin8 = y_sin[parity, pl.ds(pl.multiple_of(group * 8, 8), 8), :].astype(F32)
                for inner in range(8):
                    rows = pl.ds(pl.multiple_of(group * 512 + inner * 64, 64), 64)
                    w_scr[parity * 4 + n, rows, :] = (
                        first * cos8[inner : inner + 1] + second * sin8[inner : inner + 1]
                    ).astype(BF16)

    for parity in range(2):

        @pl.loop(0, 4)
        def _(n):
            out_ref[n, :, parity * 256 : (parity + 1) * 256] = jnp.dot(
                x_scr[parity], w_scr[parity * 4 + n], preferred_element_type=F32
            ).astype(BF16)


def planes(pair_occ, pair_emp, occupied, empty, z_first, z_second, y_cos, y_sin):
    smem = pl.BlockSpec(memory_space=pltpu.SMEM)
    vmem = pl.BlockSpec(memory_space=pltpu.VMEM)
    return pl.pallas_call(
        plane_kernel,
        out_shape=jax.ShapeDtypeStruct((4, 512, 512), BF16),
        in_specs=[smem, smem] + [vmem] * 6,
        out_specs=vmem,
        scratch_shapes=[pltpu.VMEM((2, 512, 2048), BF16), pltpu.VMEM((8, 2048, 256), BF16)],
        compiler_params=pltpu.CompilerParams(vmem_limit_bytes=LIMIT),
        name="planes",
    )(pair_occ, pair_emp, occupied, empty, z_first, z_second, y_cos, y_sin)


def x_kernel(in_ref, table_ref, out_ref, scr):
    @pl.loop(0, 32)
    def _(pair):
        rows = pl.ds(pl.multiple_of(pair * 16, 16), 16)
        stacked = jnp.concatenate(
            [
                jnp.concatenate(
                    [in_ref[n, rows, e * 256 + part * 128 : e * 256 + part * 128 + 128] for e in range(2)], 1
                )
                for part in range(2)
                for n in range(4)
            ],
            0,
        )
        waves = jnp.dot(table_ref[...], stacked, preferred_element_type=F32)
        for part in range(2):
            scr_part = scr.at[part]
            scr_part[pl.ds(pair, 64, stride=32), :] = waves[part * 64 : part * 64 + 64, 0:128]
            scr_part = scr.at[2 + part]
            scr_part[pl.ds(pair, 64, stride=32), :] = waves[part * 64 : part * 64 + 64, 128:256]

    @pl.loop(0, 16)
    def _(group):
        rows = pl.ds(pl.multiple_of(group * 128, 128), 128)
        for part in range(2):
            for e in range(2):
                out_ref[rows, (part * 2 + e) * 128 : (part * 2 + e) * 128 + 128] = scr[e * 2 + part, rows, :].astype(
                    BF16
                )


def along_x(gathered, x_table):
    vmem = pl.BlockSpec(memory_space=pltpu.VMEM)
    return pl.pallas_call(
        x_kernel,
        out_shape=jax.ShapeDtypeStruct((2048, 512), BF16),
        in_specs=[vmem] * 2,
        out_specs=vmem,
        scratch_shapes=[pltpu.VMEM((4, 2048, 128), F32)],
        compiler_params=pltpu.CompilerParams(vmem_limit_bytes=LIMIT),
        name="along_x",
    )(gathered, x_table)


def place():
    wide, narrow = lax.axis_index("wide"), lax.axis_index("narrow")
    z, x_hi, y = wide // 8, wide // 4 % 2, wide % 4
    x_lo, core = narrow // 2, narrow % 2
    return x_hi * 2 + x_lo, y, z, core


def device(x, y, z, core):
    return (z * 8 + x // 2 * 4 + y, x % 2 * 2 + core)


def sum_kernel(
    part_ref, out_ref, core_send, core_recv, acc, far_send, far_recv, near_send, near_recv,
    low_send, low_recv, z_send, z_recv, send_sem, recv_sem,
):
    x, y, z, core = place()
    mate = device(x, y, z, 1 - core)
    shifts = (
        [device((x + 1) % 4, y, z, core), device((x + 3) % 4, y, z, core)],
        [device(x, (y + 1) % 4, z, core), device(x, (y + 3) % 4, z, core)],
    )
    z_mates = [device(x, y, (z + step) % 8, core) for step in range(1, 8)]
    barrier = pltpu.get_barrier_semaphore()
    peers = [mate] + shifts[0] + shifts[1] + z_mates
    for peer in peers:
        pl.semaphore_signal(barrier, inc=1, device_id=peer, device_id_type=MESH)
    pl.semaphore_wait(barrier, len(peers))

    count = [0]
    sent = []

    def send(src, dst, peer):
        at = count[0]
        count[0] += 1
        copy = pltpu.make_async_remote_copy(
            src_ref=src, dst_ref=dst, send_sem=send_sem.at[at], recv_sem=recv_sem.at[at],
            device_id=peer, device_id_type=MESH,
        )
        copy.start()
        sent.append(copy)
        return copy

    def tile(start, size):
        return pl.ds(pl.multiple_of(start, 16), size)

    other = pl.ds(pl.multiple_of((1 - core) * 256, 256), 256)
    core_copies = []
    for piece in range(4):
        rows = pl.ds(piece * 512, 512)
        core_send[rows, :] = part_ref[rows, other].astype(BF16)
        core_copies.append(send(core_send.at[rows], core_recv.at[rows], mate))
    for piece in range(4):
        rows = pl.ds(piece * 512, 512)
        core_copies[piece].wait_recv()
        for h in range(2):
            mine = pl.ds(pl.multiple_of(core * 256 + h * 128, 128), 128)
            acc[h, rows, :] = part_ref[rows, mine] + core_recv[rows, h * 128 : h * 128 + 128].astype(F32)

    first = (x, y)
    second = (y, x)
    base = [0, 0]
    for stage in range(2):
        size = 512 if stage == 0 else 128
        half = size // 2
        me = first if stage == 0 else second
        far = {}
        start = {}
        for h in range(2):
            axis = h if stage == 0 else 1 - h
            up, down = shifts[axis]

            def block(at, h=h, me=me, size=size):
                return base[h] + (me[h] + at) % 4 * size

            start[h] = block
            far_send[stage, h, 0:half] = acc[h, tile(block(2), half), :].astype(BF16)
            far_send[stage, h, 256 : 256 + half] = acc[h, tile(block(2) + half, half), :].astype(BF16)
            far[h] = (
                send(far_send.at[stage, h, pl.ds(0, half)], far_recv.at[stage, h, pl.ds(0, half)], up),
                send(far_send.at[stage, h, pl.ds(256, half)], far_recv.at[stage, h, pl.ds(256, half)], down),
            )
        near = {}
        for h in range(2):
            axis = h if stage == 0 else 1 - h
            up, down = shifts[axis]
            block = start[h]
            near_send[stage, h, 0, half:size] = acc[h, tile(block(1) + half, half), :].astype(BF16)
            near_send[stage, h, 1, 0:half] = acc[h, tile(block(3), half), :].astype(BF16)
            far[h][0].wait_recv()
            near_send[stage, h, 0, 0:half] = (
                acc[h, tile(block(1), half), :] + far_recv[stage, h, 0:half].astype(F32)
            ).astype(BF16)
            to_up = send(near_send.at[stage, h, 0, pl.ds(0, size)], near_recv.at[stage, h, 0, pl.ds(0, size)], up)
            far[h][1].wait_recv()
            near_send[stage, h, 1, half:size] = (
                acc[h, tile(block(3) + half, half), :] + far_recv[stage, h, 256 : 256 + half].astype(F32)
            ).astype(BF16)
            to_down = send(near_send.at[stage, h, 1, pl.ds(0, size)], near_recv.at[stage, h, 1, pl.ds(0, size)], down)
            near[h] = (to_up, to_down)
        for h in range(2):
            block = start[h]
            near[h][0].wait_recv()
            near[h][1].wait_recv()
            rows = tile(block(0), size)
            acc[h, rows, :] = (
                acc[h, rows, :]
                + near_recv[stage, h, 0, 0:size].astype(F32)
                + near_recv[stage, h, 1, 0:size].astype(F32)
            )
            base[h] = block(0)

    copies = []
    for step in range(1, 8):
        for h in range(2):
            z_send[step, h] = acc[h, tile(base[h] + (z + step) % 8 * 16, 16), :].astype(BF16)
        copies.append(send(z_send.at[step], z_recv.at[step], z_mates[step - 1]))
    total = [acc[h, tile(base[h] + z * 16, 16), :] for h in range(2)]
    for step in range(1, 8):
        copies[step - 1].wait_recv()
        for h in range(2):
            total[h] = total[h] + z_recv[step, h].astype(F32)

    for h in range(2):
        low_send[h] = total[h].astype(BF16)
        out_ref[core * 2 + h, tile(base[h] + z * 16, 16), :] = low_send[h]
    copies = []
    for step in range(1, 8):
        copies.append(send(low_send, low_recv.at[step], z_mates[step - 1]))
    for step in range(1, 8):
        copies[step - 1].wait_recv()
        for h in range(2):
            out_ref[core * 2 + h, tile(base[h] + (z + 8 - step) % 8 * 16, 16), :] = low_recv[step, h]
    for stage in (1, 0):
        size = 512 if stage == 0 else 128
        half = size // 2
        me = first if stage == 0 else second
        outer = [base[h] - me[h] * size for h in range(2)]
        near = {}
        for h in range(2):
            axis = h if stage == 0 else 1 - h
            up, down = shifts[axis]
            mine = out_ref.at[core * 2 + h, tile(base[h], size)]
            near[h] = (send(mine, mine, up), send(mine, mine, down))
        far = {}
        for h in range(2):
            axis = h if stage == 0 else 1 - h
            up, down = shifts[axis]
            near[h][0].wait_recv()
            piece = out_ref.at[core * 2 + h, tile(outer[h] + (me[h] + 3) % 4 * size, half)]
            to_up = send(piece, piece, up)
            near[h][1].wait_recv()
            piece = out_ref.at[core * 2 + h, tile(outer[h] + (me[h] + 1) % 4 * size + half, half)]
            far[h] = (to_up, send(piece, piece, down))
        for h in range(2):
            far[h][0].wait_recv()
            far[h][1].wait_recv()
            base[h] = outer[h]
    for h in range(2):
        mine = out_ref.at[core * 2 + h]
        send(mine, mine, mate).wait_recv()
    for copy in sent:
        copy.wait_send()


def sum_projections(partial_term):
    vmem = pl.BlockSpec(memory_space=pltpu.VMEM)
    copies = 4 + 8 * 2 + 7 + 7 + 8 + 8 + 2
    return pl.pallas_call(
        sum_kernel,
        out_shape=jax.ShapeDtypeStruct((4, 2048, 128), BF16),
        in_specs=[vmem],
        out_specs=vmem,
        scratch_shapes=[
            pltpu.VMEM((2048, 256), BF16),
            pltpu.VMEM((2048, 256), BF16),
            pltpu.VMEM((2, 2048, 128), F32),
            pltpu.VMEM((2, 2, 512, 128), BF16),
            pltpu.VMEM((2, 2, 512, 128), BF16),
            pltpu.VMEM((2, 2, 2, 512, 128), BF16),
            pltpu.VMEM((2, 2, 2, 512, 128), BF16),
            pltpu.VMEM((2, 16, 128), BF16),
            pltpu.VMEM((8, 2, 16, 128), BF16),
            pltpu.VMEM((8, 2, 16, 128), BF16),
            pltpu.VMEM((8, 2, 16, 128), BF16),
            pltpu.SemaphoreType.DMA((copies,)),
            pltpu.SemaphoreType.DMA((copies,)),
        ],
        compiler_params=pltpu.CompilerParams(vmem_limit_bytes=LIMIT, collective_id=0, has_side_effects=True),
        name="sum_projections",
    )(partial_term)


def response_kernel(waves_ref, perm_ref, weights_ref, proj_ref, coulomb_ref, out_ref, turned):
    w = pl.program_id(0)

    @pl.when(w == 0)
    def _():
        for piece in range(4):
            turned[:, piece * 512 : piece * 512 + 512] = lax.dot_general(
                perm_ref[...],
                waves_ref[piece * 512 : piece * 512 + 512, :],
                (((1,), (1,)), ((), ())),
                preferred_element_type=F32,
            ).astype(BF16)

    lanes = lax.broadcasted_iota(jnp.int32, (256, 8), 1)
    total = jnp.zeros((512, 512), F32)
    for piece in range(8):
        rows = slice(piece * 256, piece * 256 + 256)
        column = jnp.sum(jnp.where(lanes == w, weights_ref[rows, :], 0.0), axis=1, keepdims=True)
        weighted = jnp.concatenate(
            [(proj_ref[block, rows, :].astype(F32) * column).astype(BF16) for block in range(4)], 1
        )
        total += jnp.dot(turned[:, rows], weighted, preferred_element_type=F32)
    out_ref[0] = (total * coulomb_ref[...]).astype(BF16)


def respond(waves, perm, weights, projections, coulomb):
    def whole(*shape):
        return pl.BlockSpec(shape, lambda w: (0,) * len(shape))

    return pl.pallas_call(
        response_kernel,
        out_shape=jax.ShapeDtypeStruct((8, 512, 512), BF16),
        grid=(8,),
        in_specs=[whole(2048, 512), whole(512, 512), whole(2048, 8), whole(4, 2048, 128), whole(512, 1)],
        out_specs=pl.BlockSpec((1, 512, 512), lambda w: (w, 0, 0)),
        scratch_shapes=[pltpu.VMEM((512, 2048), BF16)],
        compiler_params=pltpu.CompilerParams(vmem_limit_bytes=LIMIT),
        name="respond",
    )(waves, perm, weights, projections, coulomb)


def shards(occupied, empty, pair_occ, pair_emp, pair_level, denominators, trial):
    z_first, z_second, y_cos, y_sin, x_table, perm = [jnp.asarray(t) for t in tables()]
    blocks = planes(pair_occ, pair_emp, occupied, empty, z_first, z_second, y_cos, y_sin)
    gathered = lax.all_to_all(blocks, "narrow", split_axis=0, concat_axis=0, tiled=True)
    waves = along_x(gathered, x_table).reshape(64, 32, 512)
    columns = lax.all_to_all(waves, "wide", split_axis=0, concat_axis=0, tiled=True).reshape(2048, 512)

    freq_x = lax.axis_index("wide")
    freq_x = jnp.where(freq_x < GRID // 2, freq_x, freq_x - GRID)
    at = jnp.arange(512, dtype=jnp.int32)
    freq_y = at // 16
    freq_y = jnp.where(freq_y < GRID // 4, freq_y, freq_y - GRID // 2)
    freq_z = lax.axis_index("narrow") * 8 + at % 16 // 2
    squared = (freq_x * freq_x + freq_y * freq_y + freq_z * freq_z).astype(F32)
    quarter = float(GRID // 4)
    coulomb = (1.0 / jnp.sqrt(1.0 + squared / (quarter * quarter)))[:, None]
    scaled = (coulomb * trial.astype(F32)).astype(BF16)
    scaled = jnp.dot(perm.T, scaled, preferred_element_type=F32).astype(BF16)
    partial_term = jnp.dot(columns, scaled, preferred_element_type=F32)
    projections = sum_projections(partial_term)
    rows = jnp.arange(denominators.shape[0], dtype=jnp.int32)
    onehot = (pair_level[:, None] == rows[None, :]).astype(F32)
    weights = jnp.dot(onehot, denominators, precision=lax.Precision.HIGHEST)
    return respond(columns, perm, weights, projections, coulomb)


def solution(mesh):
    placed = (
        P("wide", "narrow", None),
        P("wide", "narrow", None),
        P("wide"),
        P("wide"),
        P(),
        P(),
        P(("wide", "narrow"), None),
    )
    return jax.shard_map(
        shards,
        mesh=mesh,
        in_specs=placed,
        out_specs=P(None, ("wide", "narrow"), None),
        check_vma=False,
    )
```

```python
import math

import jax
import jax.numpy as jnp
import ml_dtypes
import numpy as np
from jax import lax
from jax.experimental import pallas as pl
from jax.experimental.pallas import tpu as pltpu
from jax.sharding import PartitionSpec as P

GRID = 64
MESH = pl.DeviceIdType.MESH
F32, BF16 = jnp.float32, jnp.bfloat16
LIMIT = 60 * 1024 * 1024


def rounded(values):
    return values.astype(np.float32).astype(ml_dtypes.bfloat16).astype(np.float32)


def tables():
    at = np.arange(GRID)
    half = np.arange(GRID // 2)
    scaling = 1.0 / math.sqrt(GRID)
    step = 2.0 * math.pi / GRID
    z_angles = (at[:, None] * half[None, :] % GRID) * step
    z_real = rounded(scaling * np.cos(z_angles))
    z_imag = rounded(-scaling * np.sin(z_angles))
    signed = np.where(half < GRID // 4, half, half - GRID // 2)
    y_angles = (signed[:, None] * at[None, :] % GRID) * step
    y_cos = rounded(scaling * np.cos(y_angles))
    y_sin = rounded(scaling * np.sin(y_angles))
    x_angles = (at[:, None] * at[None, :] % GRID) * step
    x_cos = rounded(scaling * np.cos(x_angles))
    x_sin = rounded(scaling * np.sin(x_angles))
    zr = z_real.reshape(GRID, 4, 8).transpose(1, 0, 2)
    zi = z_imag.reshape(GRID, 4, 8).transpose(1, 0, 2)

    def spread(first, second):
        both = np.stack([first, second], 2)[:, :, :, None, :]
        return np.broadcast_to(both, (4, GRID, 2, 16, 8)).reshape(4, GRID, 256)

    z_first = spread(zr, zi)
    z_second = spread(zi, -zr)

    def widen(table):
        table = table[:, :32].reshape(16, 2, 32).transpose(1, 2, 0)
        return np.broadcast_to(table[:, :, None, :, None], (2, 32, 2, 16, 8)).reshape(2, 32, 256)

    x_table = np.block([[x_cos, x_sin], [-x_sin, x_cos]])
    perm = np.zeros((512, 512), np.float32)
    parity, part, j16, kz8 = np.meshgrid(np.arange(2), np.arange(2), np.arange(16), np.arange(8), indexing="ij")
    inner = np.arange(512)
    outer = ((2 * j16 + parity) * 16 + 2 * kz8 + part).reshape(-1)
    perm[outer, inner] = 1.0
    small = [z_first, z_second, widen(y_cos), widen(y_sin), x_table, perm, perm.T]
    return [np.ascontiguousarray(t).astype(ml_dtypes.bfloat16) for t in small]


def place():
    wide, narrow = lax.axis_index("wide"), lax.axis_index("narrow")
    z, x_hi, y = wide // 8, wide // 4 % 2, wide % 4
    x_lo, core = narrow // 2, narrow % 2
    return x_hi * 2 + x_lo, y, z, core


def device(x, y, z, core):
    return (z * 8 + x // 2 * 4 + y, x % 2 * 2 + core)


def coulomb_column():
    freq_x, narrow = lax.axis_index("wide"), lax.axis_index("narrow")
    freq_x = jnp.where(freq_x < GRID // 2, freq_x, freq_x - GRID)
    at = lax.broadcasted_iota(jnp.int32, (512, 1), 0)
    freq_y = at >> 4
    freq_y = jnp.where(freq_y < GRID // 4, freq_y, freq_y - GRID // 2)
    freq_z = narrow * 8 + ((at & 15) >> 1)
    squared = (freq_x * freq_x + freq_y * freq_y + freq_z * freq_z).astype(F32)
    quarter = float(GRID // 4)
    return 1.0 / jnp.sqrt(1.0 + squared * (1.0 / (quarter * quarter)))


def tile(start, size, unit=16):
    return pl.ds(pl.multiple_of(start, unit), size)


def main_kernel(
    occ_at, emp_at, occ_ref, emp_ref, z_first, z_second, y_cos, y_sin, x_table, perm_ref, perm_t_ref,
    level_ref, denom_ref, trial_ref,
    turned_ref, weights_ref, out_ref,
    x_scr, w_scr, blocks, gathered, columns_f32, waves, pairs, scaled, core_send, core_recv, acc,
    axis_send, axis_recv, z_send, z_recv, z_all,
    narrow_sent, narrow_got, wide_sent, wide_got, send_sem, recv_sem,
):
    wide, narrow = lax.axis_index("wide"), lax.axis_index("narrow")
    x, y, z, core = place()
    x_lo = narrow // 2
    mate = device(x, y, z, 1 - core)
    axis_mates = (
        [device((x + step) % 4, y, z, core) for step in range(1, 4)],
        [device(x, (y + step) % 4, z, core) for step in range(1, 4)],
    )
    z_mates = [device(x, y, (z + step) % 8, core) for step in range(1, 8)]

    barrier = pltpu.get_barrier_semaphore()

    @pl.loop(1, 64)
    def _(step):
        pl.semaphore_signal(barrier, inc=1, device_id=((wide + step) % 64, narrow), device_id_type=MESH)

    for step in range(1, 4):
        pl.semaphore_signal(barrier, inc=1, device_id=(wide, (narrow + step) % 4), device_id_type=MESH)
    across = device(jnp.where(x_lo == 0, (x + 3) % 4, (x + 1) % 4), y, z, core)
    pl.semaphore_signal(barrier, inc=1, device_id=across, device_id_type=MESH)

    @pl.loop(0, 32)
    def _(pair):
        product = occ_ref[occ_at[pair]].astype(F32) * emp_ref[emp_at[pair]].astype(F32)
        low, high = product[:, :2048], product[:, 2048:]
        rows = tile(pair * 16, 16)
        x_scr[0, rows, :] = (low + high).astype(BF16)
        x_scr[1, rows, :] = (low - high).astype(BF16)

    def narrow_copy(k, half, parity):
        peer = (x_lo + 1 - k // 2) % 2 * 2 + (core + (k + 1) // 2 % 2) % 2
        at = (half * 2 + parity) * 3 + k
        return pltpu.make_async_remote_copy(
            src_ref=blocks.at[k, half, parity], dst_ref=gathered.at[narrow, half, parity],
            send_sem=narrow_sent.at[at], recv_sem=narrow_got.at[at],
            device_id=(wide, peer), device_id_type=MESH,
        )

    for parity in range(2):
        for n in range(4):
            first = z_first[n].astype(F32)
            second = z_second[n].astype(F32)

            @pl.loop(0, 4)
            def _(group):
                cos8 = y_cos[parity, tile(group * 8, 8, 8), :].astype(F32)
                sin8 = y_sin[parity, tile(group * 8, 8, 8), :].astype(F32)
                for inner in range(8):
                    w_scr[n, tile(group * 512 + inner * 64, 64), :] = (
                        first * cos8[inner : inner + 1] + second * sin8[inner : inner + 1]
                    ).astype(BF16)

        if parity == 0:
            pl.semaphore_wait(barrier, 67)

        @pl.loop(0, 4)
        def _(k):
            peer = (x_lo + 1 - k // 2) % 2 * 2 + (core + (k + 1) // 2 % 2) % 2
            plane = jnp.dot(x_scr[parity], w_scr[peer], preferred_element_type=F32).astype(BF16)

            @pl.when(k < 3)
            def _():
                blocks[k, 0, parity] = plane[:256]
                blocks[k, 1, parity] = plane[256:]
                narrow_copy(k, 0, parity).start()

            @pl.when(k == 3)
            def _():
                gathered[narrow, 0, parity] = plane[:256]
                gathered[narrow, 1, parity] = plane[256:]

    for parity in range(2):
        for k in range(3):
            narrow_copy(k, 1, parity).start()

    column = coulomb_column()
    trial = (column * trial_ref[...].astype(F32)).astype(BF16)
    trial = jnp.dot(perm_t_ref[...], trial, preferred_element_type=F32).astype(BF16)
    scaled[0] = jnp.where(core == 0, trial[:, :256], trial[:, 256:])
    scaled[1] = jnp.where(core == 0, trial[:, 256:], trial[:, :256])

    def wide_copy(chunk, peer):
        return pltpu.make_async_remote_copy(
            src_ref=waves.at[chunk, peer], dst_ref=pairs.at[chunk, wide],
            send_sem=wide_sent.at[chunk], recv_sem=wide_got.at[chunk],
            device_id=(peer, narrow), device_id_type=MESH,
        )

    def wide_all(chunk):
        whole = pairs.at[chunk, pl.ds(0, 63)]
        return pltpu.make_async_remote_copy(
            src_ref=whole, dst_ref=whole, send_sem=wide_sent.at[chunk], recv_sem=wide_got.at[chunk],
            device_id=mate, device_id_type=MESH,
        )

    for chunk in range(4):
        half, parity = chunk // 2, chunk % 2
        for k in range(3):
            narrow_copy(k, half, parity).wait_recv()

        @pl.loop(0, 4)
        def _(group):
            stacked = jnp.concatenate(
                [
                    jnp.concatenate(
                        [
                            gathered[n, half, parity, tile(group * 64 + q * 16, 16), part * 128 : part * 128 + 128]
                            for q in range(4)
                        ],
                        1,
                    )
                    for part in range(2)
                    for n in range(4)
                ],
                0,
            )
            result = jnp.dot(x_table[...], stacked, preferred_element_type=F32)
            for q in range(4):
                for part in range(2):
                    columns_f32[part, pl.ds(group * 4 + q, 64, stride=16), :] = result[
                        part * 64 : part * 64 + 64, q * 128 : q * 128 + 128
                    ]

        @pl.loop(0, 8)
        def _(group):
            for part in range(2):
                waves[chunk, tile(group * 8, 8, 8), :, part * 128 : part * 128 + 128] = (
                    columns_f32[part, tile(group * 128, 128), :].astype(BF16).reshape(8, 16, 128)
                )

        @pl.loop(1, 64)
        def _(step):
            wide_copy(chunk, (wide + step) % 64).start()

        pairs[chunk, wide] = waves[chunk, wide]

    table = denom_ref[...]
    onehot = (lax.broadcasted_iota(jnp.int32, (NTAB, 2048), 0) == level_ref[...]).astype(F32).astype(BF16)
    picked = jnp.zeros((2048, 128), F32)
    for _ in range(3):
        piece = table.astype(BF16)
        table = table - piece.astype(F32)
        picked += lax.dot_general(onehot, piece, (((0,), (0,)), ((), ())), preferred_element_type=F32)
    picked = picked.reshape(64, 2, 16, 128)
    for half in range(2):
        weights_ref[half] = picked[:, half].reshape(1024, 128)

    count = [0]
    sent = []

    def send(src, dst, peer):
        at = count[0]
        count[0] += 1
        copy = pltpu.make_async_remote_copy(
            src_ref=src, dst_ref=dst, send_sem=send_sem.at[at], recv_sem=recv_sem.at[at],
            device_id=peer, device_id_type=MESH,
        )
        copy.start()
        sent.append(copy)
        return copy

    def project(half, which, rows):
        return jnp.dot(
            pairs[half * 2, pl.ds(rows, 16)].reshape(256, 256), scaled[which, 0:256],
            preferred_element_type=F32,
        ) + jnp.dot(
            pairs[half * 2 + 1, pl.ds(rows, 16)].reshape(256, 256), scaled[which, 256:512],
            preferred_element_type=F32,
        )

    def turn(half):
        @pl.loop(0, 2)
        def _(piece):
            total = jnp.zeros((512, 512), F32)
            for parity in range(2):
                total += lax.dot_general(
                    perm_ref[:, parity * 256 : parity * 256 + 256],
                    pairs[half * 2 + parity, tile(piece * 32, 32)].reshape(512, 256),
                    (((1,), (1,)), ((), ())),
                    preferred_element_type=F32,
                )
            turned_ref[half * 2 + piece] = total.astype(BF16)

    def reduce(half):
        for parity in range(2):
            wide_all(half * 2 + parity).wait_recv()
        copies = []
        for piece in range(4):
            rows = pl.ds(piece * 256, 256)
            core_send[half, rows, :] = project(half, 1, piece * 16).astype(BF16)
            copies.append(send(core_send.at[half, rows], core_recv.at[half, rows], mate))
        for piece in range(4):
            own = project(half, 0, piece * 16)
            acc[half, 0, piece * 256 : piece * 256 + 256, :] = own[:, :128]
            acc[half, 1, piece * 256 : piece * 256 + 256, :] = own[:, 128:]
        yield
        for piece in range(4):
            rows = pl.ds(piece * 256, 256)
            copies[piece].wait_recv()
            for h in range(2):
                acc[half, h, rows, :] += core_recv[half, rows, h * 128 : h * 128 + 128].astype(F32)
        base = [0, 0]
        places = ((x, y), (y, x))
        for stage in range(2):
            size = 256 if stage == 0 else 64
            copies = {}
            for h in range(2):
                for step in range(1, 4):
                    rows = tile(base[h] + (places[stage][h] + step) % 4 * size, size)
                    axis_send[half, stage, h, step, 0:size] = acc[half, h, rows, :].astype(BF16)
                    copies[h, step] = send(
                        axis_send.at[half, stage, h, step, pl.ds(0, size)],
                        axis_recv.at[half, stage, h, step, pl.ds(0, size)],
                        axis_mates[(h + stage) % 2][step - 1],
                    )
            yield
            for h in range(2):
                for step in range(1, 4):
                    copies[h, step].wait_recv()
                base[h] = base[h] + places[stage][h] * size
                rows = tile(base[h], size)
                total = acc[half, h, rows, :]
                for step in range(1, 4):
                    total += axis_recv[half, stage, h, step, 0:size].astype(F32)
                acc[half, h, rows, :] = total
        copies = []
        for step in range(1, 8):
            for h in range(2):
                z_send[half, step, h] = acc[half, h, tile(base[h] + (z + step) % 8 * 8, 8, 8), :]
            copies.append(send(z_send.at[half, step], z_recv.at[half, step], z_mates[step - 1]))
        yield
        for copy in copies:
            copy.wait_recv()
        for h in range(2):
            total = acc[half, h, tile(base[h] + z * 8, 8, 8), :]
            for step in range(1, 8):
                total += z_recv[half, step, h]
            z_all[half, z, h] = total
        mine = z_all.at[half, z]
        copies = [send(mine, mine, peer) for peer in z_mates]
        yield
        for copy in copies:
            copy.wait_recv()
        for h in range(2):
            out_ref[core * 2 + h, tile(half * 1024 + base[h], 64), :] = (
                z_all[half, :, h].reshape(64, 128).astype(BF16)
            )
        for stage in (1, 0):
            size = 256 if stage == 0 else 64
            copies = {}
            for h in range(2):
                mine = out_ref.at[core * 2 + h, tile(half * 1024 + base[h], size)]
                for step in range(1, 4):
                    copies[h, step] = send(mine, mine, axis_mates[(h + stage) % 2][step - 1])
            last = []
            if stage == 0:
                for h in range(2):
                    mine = out_ref.at[core * 2 + h, tile(half * 1024 + base[h], size)]
                    last.append(send(mine, mine, mate))
            yield
            for step in range(1, 4):
                for h in range(2):
                    copies[h, step].wait_recv()
                    if stage == 0:
                        start = half * 1024 + (places[0][h] + 4 - step) % 4 * 256
                        piece = out_ref.at[core * 2 + h, tile(start, 256)]
                        last.append(send(piece, piece, mate))
            for h in range(2):
                base[h] = base[h] - places[stage][h] * size
        yield
        for copy in last:
            copy.wait_recv()

    runs = [reduce(half) for half in range(2)]
    if LOCKSTEP:
        next(runs[0])
        turn(0)
        next(runs[1])
        turn(1)
        alive = runs
        while alive:
            alive = [run for run in alive if next(run, 1) is None]
    else:
        next(runs[0])
        turn(0)
        for _ in runs[0]:
            pass
        next(runs[1])
        turn(1)
        for _ in runs[1]:
            pass

    for parity in range(2):
        for half in range(2):
            for k in range(3):
                narrow_copy(k, half, parity).wait_send()
    for chunk in range(4):
        wide_all(chunk).wait_send()
    for copy in sent:
        copy.wait_send()


LOCKSTEP = True
NTAB = 64


def main(pair_occ, pair_emp, *arrays):
    smem = pl.BlockSpec(memory_space=pltpu.SMEM)
    vmem = pl.BlockSpec(memory_space=pltpu.VMEM)
    copies = 2 * (4 + 12 + 7 + 7 + 12 + 8)
    dma = pltpu.SemaphoreType.DMA
    return pl.pallas_call(
        main_kernel,
        out_shape=(
            jax.ShapeDtypeStruct((4, 512, 512), BF16),
            jax.ShapeDtypeStruct((2, 1024, 128), F32),
            jax.ShapeDtypeStruct((4, 2048, 128), BF16),
        ),
        in_specs=[smem, smem] + [vmem] * len(arrays),
        out_specs=(vmem, vmem, vmem),
        scratch_shapes=[
            pltpu.VMEM((2, 512, 2048), BF16),
            pltpu.VMEM((4, 2048, 256), BF16),
            pltpu.VMEM((3, 2, 2, 256, 256), BF16),
            pltpu.VMEM((4, 2, 2, 256, 256), BF16),
            pltpu.VMEM((2, 1024, 128), F32),
            pltpu.VMEM((4, 64, 16, 256), BF16),
            pltpu.VMEM((4, 64, 16, 256), BF16),
            pltpu.VMEM((2, 512, 256), BF16),
            pltpu.VMEM((2, 1024, 256), BF16),
            pltpu.VMEM((2, 1024, 256), BF16),
            pltpu.VMEM((2, 2, 1024, 128), F32),
            pltpu.VMEM((2, 2, 2, 4, 256, 128), BF16),
            pltpu.VMEM((2, 2, 2, 4, 256, 128), BF16),
            pltpu.VMEM((2, 8, 2, 8, 128), F32),
            pltpu.VMEM((2, 8, 2, 8, 128), F32),
            pltpu.VMEM((2, 8, 2, 8, 128), F32),
            dma((12,)), dma((12,)), dma((4,)), dma((4,)), dma((copies,)), dma((copies,)),
        ],
        compiler_params=pltpu.CompilerParams(vmem_limit_bytes=LIMIT, collective_id=0, has_side_effects=True),
        name="main",
    )(pair_occ, pair_emp, *arrays)


def response_kernel(turned_ref, weights_ref, proj_ref, out_ref):
    w = pl.program_id(0)
    total = jnp.zeros((512, 512), F32)
    for piece in range(8):
        rows = slice(piece * 256, piece * 256 + 256)
        weights = weights_ref[rows, :]
        column = pltpu.roll(weights, (128 - w) % 128, 1)[:, 0:1]
        weighted = jnp.concatenate(
            [(proj_ref[block, rows, :].astype(F32) * column).astype(BF16) for block in range(4)], 1
        )
        at = piece % 2 * 256
        total += jnp.dot(turned_ref[piece // 2, :, at : at + 256], weighted, preferred_element_type=F32)
    out_ref[0] = (total * coulomb_column()).astype(BF16)


def respond(turned, weights, projections):
    def whole(*shape):
        return pl.BlockSpec(shape, lambda w: (0,) * len(shape))

    return pl.pallas_call(
        response_kernel,
        out_shape=jax.ShapeDtypeStruct((8, 512, 512), BF16),
        grid=(8,),
        in_specs=[whole(4, 512, 512), whole(2048, 128), whole(4, 2048, 128)],
        out_specs=pl.BlockSpec((1, 512, 512), lambda w: (w, 0, 0)),
        compiler_params=pltpu.CompilerParams(vmem_limit_bytes=LIMIT),
        name="respond",
    )(turned, weights, projections)


def shards(occupied, empty, pair_occ, pair_emp, pair_level, denominators, trial):
    constants = [jnp.asarray(t) for t in tables()]
    turned, weights, projections = main(
        pair_occ, pair_emp, occupied, empty, *constants,
        pair_level.reshape(1, 2048), jnp.pad(denominators, ((0, 0), (0, 120))), trial,
    )
    return respond(turned, weights.reshape(2048, 128), projections)


def solution(mesh):
    placed = (
        P("wide", "narrow", None),
        P("wide", "narrow", None),
        P("wide"),
        P("wide"),
        P(),
        P(),
        P(("wide", "narrow"), None),
    )
    return jax.shard_map(
        shards,
        mesh=mesh,
        in_specs=placed,
        out_specs=P(None, ("wide", "narrow"), None),
        check_vma=False,
    )
```

```python
import math

import jax
import jax.numpy as jnp
import ml_dtypes
import numpy as np
from jax import lax
from jax.experimental import pallas as pl
from jax.experimental.pallas import tpu as pltpu
from jax.sharding import PartitionSpec as P

GRID = 64
MESH = pl.DeviceIdType.MESH
F32, BF16 = jnp.float32, jnp.bfloat16
MAIN_LIMIT = 62 * 1024 * 1024
RESPOND_LIMIT = 60 * 1024 * 1024


def rounded(values):
    return values.astype(np.float32).astype(ml_dtypes.bfloat16).astype(np.float32)


def tables():
    at = np.arange(GRID)
    half = np.arange(GRID // 2)
    scaling = 1.0 / math.sqrt(GRID)
    step = 2.0 * math.pi / GRID
    z_angles = (at[:, None] * half[None, :] % GRID) * step
    z_real = rounded(scaling * np.cos(z_angles))
    z_imag = rounded(-scaling * np.sin(z_angles))
    signed = np.where(half < GRID // 4, half, half - GRID // 2)
    y_angles = (signed[:, None] * at[None, :] % GRID) * step
    y_cos = rounded(scaling * np.cos(y_angles))
    y_sin = rounded(scaling * np.sin(y_angles))
    x_angles = (at[:, None] * at[None, :] % GRID) * step
    x_cos = rounded(scaling * np.cos(x_angles))
    x_sin = rounded(scaling * np.sin(x_angles))
    zr = z_real.reshape(GRID, 4, 8).transpose(1, 0, 2)
    zi = z_imag.reshape(GRID, 4, 8).transpose(1, 0, 2)

    def spread(first, second):
        both = np.stack([first, second], 2)[:, :, :, None, :]
        return np.broadcast_to(both, (4, GRID, 2, 16, 8)).reshape(4, GRID, 256)

    z_first = spread(zr, zi)
    z_second = spread(zi, -zr)

    def widen(table):
        table = table[:, :32].reshape(16, 2, 32).transpose(1, 2, 0)
        return np.broadcast_to(table[:, :, None, :, None], (2, 32, 2, 16, 8)).reshape(2, 32, 256)

    x_table = np.block([[x_cos, x_sin], [-x_sin, x_cos]])
    perm = np.zeros((512, 512), np.float32)
    parity, part, j16, kz8 = np.meshgrid(np.arange(2), np.arange(2), np.arange(16), np.arange(8), indexing="ij")
    inner = np.arange(512)
    outer = ((2 * j16 + parity) * 16 + 2 * kz8 + part).reshape(-1)
    perm[outer, inner] = 1.0
    small = [z_first, z_second, widen(y_cos), widen(y_sin), x_table, perm, perm.T]
    return [np.ascontiguousarray(t).astype(ml_dtypes.bfloat16) for t in small]


def place():
    wide, narrow = lax.axis_index("wide"), lax.axis_index("narrow")
    z, x_hi, y = wide // 8, wide // 4 % 2, wide % 4
    x_lo, core = narrow // 2, narrow % 2
    return x_hi * 2 + x_lo, y, z, core


def device(x, y, z, core):
    return (z * 8 + x // 2 * 4 + y, x % 2 * 2 + core)


def coulomb_column():
    freq_x, narrow = lax.axis_index("wide"), lax.axis_index("narrow")
    freq_x = jnp.where(freq_x < GRID // 2, freq_x, freq_x - GRID)
    at = lax.broadcasted_iota(jnp.int32, (512, 1), 0)
    freq_y = at >> 4
    freq_y = jnp.where(freq_y < GRID // 4, freq_y, freq_y - GRID // 2)
    freq_z = narrow * 8 + ((at & 15) >> 1)
    squared = (freq_x * freq_x + freq_y * freq_y + freq_z * freq_z).astype(F32)
    quarter = float(GRID // 4)
    return 1.0 / jnp.sqrt(1.0 + squared * (1.0 / (quarter * quarter)))


def tile(start, size, unit=16):
    return pl.ds(pl.multiple_of(start, unit), size)


def weigh(w, weights_ref, proj_ref):
    column = pltpu.roll(weights_ref[0], (128 - w) % 128, 1)[:, 0:1]
    return jnp.concatenate(
        [(proj_ref[block, 0:1024].astype(F32) * column).astype(BF16) for block in range(4)], 1
    )


def main_kernel(
    occ_at, emp_at, occ_ref, emp_ref, z_first, z_second, y_cos, y_sin, x_table, perm_hbm, perm_t_hbm,
    level_ref, denom_ref, trial_hbm,
    turned_ref, weights_ref, out_ref, early_hbm, early, early_sem,
    trial_ref, perm_ref, perm_t_ref, late_sem, x_scr, w_scr, blocks, gathered, columns_f32, waves, pairs, scaled, core_send, core_recv, acc,
    axis_send, axis_recv, z_send, z_recv, z_all,
    narrow_sent, narrow_got, wide_sent, wide_got, send_sem, recv_sem,
):
    wide, narrow = lax.axis_index("wide"), lax.axis_index("narrow")
    x, y, z, core = place()
    x_lo = narrow // 2
    mate = device(x, y, z, 1 - core)
    axis_mates = (
        [device((x + step) % 4, y, z, core) for step in range(1, 4)],
        [device(x, (y + step) % 4, z, core) for step in range(1, 4)],
    )
    z_mates = [device(x, y, (z + step) % 8, core) for step in range(1, 8)]

    barrier = pltpu.get_barrier_semaphore()

    @pl.loop(1, 64)
    def _(step):
        pl.semaphore_signal(barrier, inc=1, device_id=((wide + step) % 64, narrow), device_id_type=MESH)

    for step in range(1, 4):
        pl.semaphore_signal(barrier, inc=1, device_id=(wide, (narrow + step) % 4), device_id_type=MESH)
    across = device(jnp.where(x_lo == 0, (x + 3) % 4, (x + 1) % 4), y, z, core)
    pl.semaphore_signal(barrier, inc=1, device_id=across, device_id_type=MESH)

    late = [
        pltpu.make_async_copy(src, dst, late_sem.at[at])
        for at, (src, dst) in enumerate(((trial_hbm, trial_ref), (perm_hbm, perm_ref), (perm_t_hbm, perm_t_ref)))
    ]
    for copy in late:
        copy.start()

    def products(half):
        @pl.loop(half * 16, half * 16 + 16)
        def _(pair):
            product = occ_ref[occ_at[pair]] * emp_ref[emp_at[pair]]
            low, high = product[:, :2048], product[:, 2048:]
            rows = tile(pair * 16, 16)
            x_scr[0, rows, :] = low + high
            x_scr[1, rows, :] = low - high

    def narrow_copy(k, half, parity):
        peer = (x_lo + 1 - k // 2) % 2 * 2 + (core + (k + 1) // 2 % 2) % 2
        at = (half * 2 + parity) * 3 + k
        return pltpu.make_async_remote_copy(
            src_ref=blocks.at[k, half, parity], dst_ref=gathered.at[narrow, half, parity],
            send_sem=narrow_sent.at[at], recv_sem=narrow_got.at[at],
            device_id=(wide, peer), device_id_type=MESH,
        )

    def make_table(parity, n):
        first = z_first[n]
        second = z_second[n]

        @pl.loop(0, 2)
        def _(group):
            cos8 = y_cos[parity, tile(group * 16, 16), :]
            sin8 = y_sin[parity, tile(group * 16, 16), :]
            for inner in range(16):
                w_scr[parity * 4 + n, tile(group * 1024 + inner * 64, 64), :] = (
                    first * cos8[inner : inner + 1] + second * sin8[inner : inner + 1]
                )

    def planes(half, parity):
        @pl.loop(0, 4)
        def _(k):
            peer = (x_lo + 1 - k // 2) % 2 * 2 + (core + (k + 1) // 2 % 2) % 2
            if half == 0:
                make_table(parity, peer)
            plane = jnp.dot(
                x_scr[parity, half * 256 : half * 256 + 256], w_scr[parity * 4 + peer], preferred_element_type=F32
            ).astype(BF16)

            @pl.when(k < 3)
            def _():
                blocks[k, half, parity] = plane
                narrow_copy(k, half, parity).start()

            @pl.when(k == 3)
            def _():
                gathered[narrow, half, parity] = plane

    def wide_copy(chunk, peer):
        return pltpu.make_async_remote_copy(
            src_ref=waves.at[chunk, peer], dst_ref=pairs.at[chunk, wide],
            send_sem=wide_sent.at[chunk], recv_sem=wide_got.at[chunk],
            device_id=(peer, narrow), device_id_type=MESH,
        )

    def wide_all(chunk):
        whole = pairs.at[chunk, pl.ds(0, 63)]
        return pltpu.make_async_remote_copy(
            src_ref=whole, dst_ref=whole, send_sem=wide_sent.at[chunk], recv_sem=wide_got.at[chunk],
            device_id=mate, device_id_type=MESH,
        )

    def along_x(chunk):
        half, parity = chunk // 2, chunk % 2
        for k in range(3):
            narrow_copy(k, half, parity).wait_recv()

        @pl.loop(0, 4)
        def _(group):
            stacked = jnp.concatenate(
                [
                    jnp.concatenate(
                        [
                            gathered[n, half, parity, tile(group * 64 + q * 16, 16), part * 128 : part * 128 + 128]
                            for q in range(4)
                        ],
                        1,
                    )
                    for part in range(2)
                    for n in range(4)
                ],
                0,
            )
            result = jnp.dot(x_table[...], stacked, preferred_element_type=F32)
            for q in range(4):
                for part in range(2):
                    columns_f32[part, pl.ds(group * 4 + q, 64, stride=16), :] = result[
                        part * 64 : part * 64 + 64, q * 128 : q * 128 + 128
                    ]

        @pl.loop(0, 8)
        def _(group):
            for part in range(2):
                waves[chunk, tile(group * 8, 8, 8), :, part * 128 : part * 128 + 128] = (
                    columns_f32[part, tile(group * 128, 128), :].astype(BF16).reshape(8, 16, 128)
                )

        @pl.loop(1, 64, unroll=7)
        def _(step):
            wide_copy(chunk, jnp.bitwise_and(wide + step, 63)).start()

        pairs[chunk, wide] = waves[chunk, wide]

    products(0)
    pl.semaphore_wait(barrier, 67)
    planes(0, 0)
    planes(0, 1)
    products(1)
    planes(1, 0)
    planes(1, 1)
    for chunk in range(4):
        along_x(chunk)

    for copy in late:
        copy.wait()
    column = coulomb_column()
    trial = (column * trial_ref[...].astype(F32)).astype(BF16)
    trial = jnp.dot(perm_t_ref[...], trial, preferred_element_type=F32).astype(BF16)
    scaled[0] = jnp.where(core == 0, trial[:, :256], trial[:, 256:])
    scaled[1] = jnp.where(core == 0, trial[:, 256:], trial[:, :256])

    table = denom_ref[...]
    lanes = lax.broadcasted_iota(jnp.int32, (8, 128), 1)
    spread = (lax.broadcasted_iota(jnp.int32, (8, 128), 0) == lanes).astype(F32).astype(BF16)
    onehot = (lax.broadcasted_iota(jnp.int32, (NTAB, 2048), 0) == level_ref[...].reshape(1, 2048)).astype(F32).astype(BF16)
    picked = jnp.zeros((2048, 128), F32)
    for _ in range(3):
        piece = table.astype(BF16)
        table = table - piece.astype(F32)
        piece = lax.dot_general(
            piece, spread, (((0,), (0,)), ((), ())), preferred_element_type=F32
        ).astype(BF16)
        picked += lax.dot_general(onehot, piece, (((0,), (0,)), ((), ())), preferred_element_type=F32)
    picked = picked.reshape(64, 2, 16, 128)
    for half in range(2):
        weights_ref[half] = picked[:, half].reshape(1024, 128)

    count = [0]
    sent = []

    def send(src, dst, peer):
        at = count[0]
        count[0] += 1
        copy = pltpu.make_async_remote_copy(
            src_ref=src, dst_ref=dst, send_sem=send_sem.at[at], recv_sem=recv_sem.at[at],
            device_id=peer, device_id_type=MESH,
        )
        copy.start()
        sent.append(copy)
        return copy

    def project(half, which, rows):
        return jnp.dot(
            pairs[half * 2, pl.ds(rows, 16)].reshape(256, 256), scaled[which, 0:256],
            preferred_element_type=F32,
        ) + jnp.dot(
            pairs[half * 2 + 1, pl.ds(rows, 16)].reshape(256, 256), scaled[which, 256:512],
            preferred_element_type=F32,
        )

    def turn(half):
        @pl.loop(0, 2)
        def _(piece):
            total = jnp.zeros((512, 512), F32)
            for parity in range(2):
                total += lax.dot_general(
                    perm_ref[:, parity * 256 : parity * 256 + 256],
                    pairs[half * 2 + parity, tile(piece * 32, 32)].reshape(512, 256),
                    (((1,), (1,)), ((), ())),
                    preferred_element_type=F32,
                )
            turned_ref[half, :, tile(piece * 512, 512, 512)] = total.astype(BF16)

    def reduce(half):
        for parity in range(2):
            wide_all(half * 2 + parity).wait_recv()
        copies = []
        for piece in range(4):
            rows = pl.ds(piece * 256, 256)
            core_send[half, rows, :] = project(half, 1, piece * 16).astype(BF16)
            copies.append(send(core_send.at[half, rows], core_recv.at[half, rows], mate))
        for piece in range(4):
            own = project(half, 0, piece * 16)
            acc[half, 0, piece * 256 : piece * 256 + 256, :] = own[:, :128]
            acc[half, 1, piece * 256 : piece * 256 + 256, :] = own[:, 128:]
        yield
        for piece in range(4):
            rows = pl.ds(piece * 256, 256)
            copies[piece].wait_recv()
            for h in range(2):
                acc[half, h, rows, :] += core_recv[half, rows, h * 128 : h * 128 + 128].astype(F32)
        base = [0, 0]
        places = ((x, y), (y, x))
        for stage in range(2):
            size = 256 if stage == 0 else 64
            copies = {}
            for h in range(2):
                for step in range(1, 4):
                    rows = tile(base[h] + (places[stage][h] + step) % 4 * size, size)
                    axis_send[half, stage, h, step, 0:size] = acc[half, h, rows, :].astype(BF16)
                    copies[h, step] = send(
                        axis_send.at[half, stage, h, step, pl.ds(0, size)],
                        axis_recv.at[half, stage, h, step, pl.ds(0, size)],
                        axis_mates[(h + stage) % 2][step - 1],
                    )
            yield
            for h in range(2):
                for step in range(1, 4):
                    copies[h, step].wait_recv()
                base[h] = base[h] + places[stage][h] * size
                rows = tile(base[h], size)
                total = acc[half, h, rows, :]
                for step in range(1, 4):
                    total += axis_recv[half, stage, h, step, 0:size].astype(F32)
                acc[half, h, rows, :] = total
        copies = []
        for step in range(1, 8):
            for h in range(2):
                z_send[half, step, h] = acc[half, h, tile(base[h] + (z + step) % 8 * 8, 8, 8), :]
            copies.append(send(z_send.at[half, step], z_recv.at[half, step], z_mates[step - 1]))
        yield
        for copy in copies:
            copy.wait_recv()
        for h in range(2):
            total = acc[half, h, tile(base[h] + z * 8, 8, 8), :]
            for step in range(1, 8):
                total += z_recv[half, step, h]
            z_all[half, z, h] = total
        mine = z_all.at[half, z]
        copies = [send(mine, mine, peer) for peer in z_mates]
        yield
        for copy in copies:
            copy.wait_recv()
        for h in range(2):
            out_ref[core * 2 + h, tile(half * 1024 + base[h], 64), :] = (
                z_all[half, :, h].reshape(64, 128).astype(BF16)
            )
        for stage in (1, 0):
            size = 256 if stage == 0 else 64
            copies = {}
            for h in range(2):
                mine = out_ref.at[core * 2 + h, tile(half * 1024 + base[h], size)]
                for step in range(1, 4):
                    copies[h, step] = send(mine, mine, axis_mates[(h + stage) % 2][step - 1])
            last = []
            if stage == 0:
                for h in range(2):
                    mine = out_ref.at[core * 2 + h, tile(half * 1024 + base[h], size)]
                    last.append(send(mine, mine, mate))
            yield
            for step in range(1, 4):
                for h in range(2):
                    copies[h, step].wait_recv()
                    if stage == 0:
                        start = half * 1024 + (places[0][h] + 4 - step) % 4 * 256
                        piece = out_ref.at[core * 2 + h, tile(start, 256)]
                        last.append(send(piece, piece, mate))
            for h in range(2):
                base[h] = base[h] - places[stage][h] * size
        yield
        for copy in last:
            copy.wait_recv()

    runs = [reduce(half) for half in range(2)]
    def response_copy(w):
        return pltpu.make_async_copy(early.at[w], early_hbm.at[w], early_sem.at[w])

    def respond_early(first, last):
        @pl.loop(first, last)
        def _(w):
            weighted = weigh(w, weights_ref, out_ref)
            early[w] = jnp.dot(turned_ref[0], weighted, preferred_element_type=F32).astype(BF16)
            response_copy(w).start()

    next(runs[0])
    turn(0)
    for _ in range(3):
        next(runs[0])
    next(runs[1])
    turn(1)
    for _ in range(4):
        next(runs[0])
        next(runs[1])
    for _ in runs[0]:
        pass
    respond_early(0, 3)
    next(runs[1])
    respond_early(3, 5)
    next(runs[1])
    respond_early(5, 8)
    for _ in runs[1]:
        pass
    for w in range(8):
        response_copy(w).wait()

    for parity in range(2):
        for half in range(2):
            for k in range(3):
                narrow_copy(k, half, parity).wait_send()
    for chunk in range(4):
        wide_all(chunk).wait_send()
    for copy in sent:
        copy.wait_send()


NTAB = 64


def main(pair_occ, pair_emp, *arrays):
    smem = pl.BlockSpec(memory_space=pltpu.SMEM)
    vmem = pl.BlockSpec(memory_space=pltpu.VMEM)
    hbm = pl.BlockSpec(memory_space=pl.ANY)
    copies = 2 * (4 + 12 + 7 + 7 + 12 + 8)
    dma = pltpu.SemaphoreType.DMA
    return pl.pallas_call(
        main_kernel,
        out_shape=(
            jax.ShapeDtypeStruct((2, 512, 1024), BF16),
            jax.ShapeDtypeStruct((2, 1024, 128), F32),
            jax.ShapeDtypeStruct((4, 2048, 128), BF16),
            jax.ShapeDtypeStruct((8, 512, 512), BF16),
        ),
        in_specs=[smem, smem] + [vmem] * 7 + [hbm] * 2 + [vmem] * 2 + [hbm],
        out_specs=(vmem, vmem, vmem, hbm),
        scratch_shapes=[
            pltpu.VMEM((8, 512, 512), BF16),
            dma((8,)),
            pltpu.VMEM((512, 512), BF16),
            pltpu.VMEM((512, 512), BF16),
            pltpu.VMEM((512, 512), BF16),
            dma((3,)),
            pltpu.VMEM((2, 512, 2048), BF16),
            pltpu.VMEM((8, 2048, 256), BF16),
            pltpu.VMEM((3, 2, 2, 256, 256), BF16),
            pltpu.VMEM((4, 2, 2, 256, 256), BF16),
            pltpu.VMEM((2, 1024, 128), F32),
            pltpu.VMEM((4, 64, 16, 256), BF16),
            pltpu.VMEM((4, 64, 16, 256), BF16),
            pltpu.VMEM((2, 512, 256), BF16),
            pltpu.VMEM((2, 1024, 256), BF16),
            pltpu.VMEM((2, 1024, 256), BF16),
            pltpu.VMEM((2, 2, 1024, 128), F32),
            pltpu.VMEM((2, 2, 2, 4, 256, 128), BF16),
            pltpu.VMEM((2, 2, 2, 4, 256, 128), BF16),
            pltpu.VMEM((2, 8, 2, 8, 128), F32),
            pltpu.VMEM((2, 8, 2, 8, 128), F32),
            pltpu.VMEM((2, 8, 2, 8, 128), F32),
            dma((12,)), dma((12,)), dma((4,)), dma((4,)), dma((copies,)), dma((copies,)),
        ],
        compiler_params=pltpu.CompilerParams(vmem_limit_bytes=MAIN_LIMIT, collective_id=0, has_side_effects=True),
        name="main",
    )(pair_occ, pair_emp, *arrays)


def response_kernel(early_ref, turned_ref, weights_ref, proj_ref, out_ref, even, odd):
    step = pl.program_id(0)
    column = coulomb_column()

    @pl.when(step == 0)
    def _():
        even[...] = weigh(0, weights_ref, proj_ref)

    for at, (now, later) in enumerate(((even, odd), (odd, even))):
        total = early_ref[at].astype(F32) + jnp.dot(turned_ref[0], now[...], preferred_element_type=F32)
        later[...] = weigh(step * 2 + at + 1, weights_ref, proj_ref)
        out_ref[at] = (total * column).astype(BF16)


def respond(early, turned, weights, projections):
    return pl.pallas_call(
        response_kernel,
        out_shape=jax.ShapeDtypeStruct((8, 512, 512), BF16),
        grid=(4,),
        in_specs=[
            pl.BlockSpec((2, 512, 512), lambda w: (w, 0, 0)),
            pl.BlockSpec((1, 512, 1024), lambda w: (1, 0, 0)),
            pl.BlockSpec((1, 1024, 128), lambda w: (1, 0, 0)),
            pl.BlockSpec((4, 1024, 128), lambda w: (0, 1, 0)),
        ],
        out_specs=pl.BlockSpec((2, 512, 512), lambda w: (w, 0, 0)),
        scratch_shapes=[pltpu.VMEM((1024, 512), BF16), pltpu.VMEM((1024, 512), BF16)],
        compiler_params=pltpu.CompilerParams(vmem_limit_bytes=RESPOND_LIMIT),
        name="respond",
    )(early, turned, weights, projections)


def shards(occupied, empty, pair_occ, pair_emp, pair_level, denominators, trial):
    constants = [jnp.asarray(t) for t in tables()]
    turned, weights, projections, early = main(
        pair_occ, pair_emp, occupied, empty, *constants,
        pair_level, denominators.T, trial,
    )
    return respond(early, turned, weights, projections)


def solution(mesh):
    placed = (
        P("wide", "narrow", None),
        P("wide", "narrow", None),
        P("wide"),
        P("wide"),
        P(),
        P(),
        P(("wide", "narrow"), None),
    )
    return jax.shard_map(
        shards,
        mesh=mesh,
        in_specs=placed,
        out_specs=P(None, ("wide", "narrow"), None),
        check_vma=False,
    )
```

```python
import math

import jax
import jax.numpy as jnp
import ml_dtypes
import numpy as np
from jax import lax
from jax.experimental import pallas as pl
from jax.experimental.pallas import tpu as pltpu
from jax.sharding import PartitionSpec as P

GRID = 64
MESH = pl.DeviceIdType.MESH
F32, BF16 = jnp.float32, jnp.bfloat16
MAIN_LIMIT = 62 * 1024 * 1024
RESPOND_LIMIT = 60 * 1024 * 1024


def rounded(values):
    return values.astype(np.float32).astype(ml_dtypes.bfloat16).astype(np.float32)


def tables():
    at = np.arange(GRID)
    half = np.arange(GRID // 2)
    scaling = 1.0 / math.sqrt(GRID)
    step = 2.0 * math.pi / GRID
    z_angles = (at[:, None] * half[None, :] % GRID) * step
    z_real = rounded(scaling * np.cos(z_angles))
    z_imag = rounded(-scaling * np.sin(z_angles))
    signed = np.where(half < GRID // 4, half, half - GRID // 2)
    y_angles = (signed[:, None] * at[None, :] % GRID) * step
    y_cos = rounded(scaling * np.cos(y_angles))
    y_sin = rounded(scaling * np.sin(y_angles))
    x_angles = (at[:, None] * at[None, :] % GRID) * step
    x_cos = rounded(scaling * np.cos(x_angles))
    x_sin = rounded(scaling * np.sin(x_angles))
    zr = z_real.reshape(GRID, 4, 8).transpose(1, 0, 2)
    zi = z_imag.reshape(GRID, 4, 8).transpose(1, 0, 2)

    def spread(first, second):
        both = np.stack([first, second], 2)[:, :, :, None, :]
        return np.broadcast_to(both, (4, GRID, 2, 16, 8)).reshape(4, GRID, 256)

    z_first = spread(zr, zi)
    z_second = spread(zi, -zr)

    def widen(table):
        table = table[:, :32].reshape(16, 2, 32).transpose(1, 2, 0)
        return np.broadcast_to(table[:, :, None, :, None], (2, 32, 2, 16, 8)).reshape(2, 32, 256)

    x_table = np.block([[x_cos, x_sin], [-x_sin, x_cos]])
    perm = np.zeros((512, 512), np.float32)
    parity, part, j16, kz8 = np.meshgrid(np.arange(2), np.arange(2), np.arange(16), np.arange(8), indexing="ij")
    inner = np.arange(512)
    outer = ((2 * j16 + parity) * 16 + 2 * kz8 + part).reshape(-1)
    perm[outer, inner] = 1.0
    small = [z_first, z_second, widen(y_cos), widen(y_sin), x_table, perm, perm.T]
    return [np.ascontiguousarray(t).astype(ml_dtypes.bfloat16) for t in small]


def place():
    wide, narrow = lax.axis_index("wide"), lax.axis_index("narrow")
    z, x_hi, y = wide // 8, wide // 4 % 2, wide % 4
    x_lo, core = narrow // 2, narrow % 2
    return x_hi * 2 + x_lo, y, z, core


def device(x, y, z, core):
    return (z * 8 + x // 2 * 4 + y, x % 2 * 2 + core)


def coulomb_column():
    freq_x, narrow = lax.axis_index("wide"), lax.axis_index("narrow")
    freq_x = jnp.where(freq_x < GRID // 2, freq_x, freq_x - GRID)
    at = lax.broadcasted_iota(jnp.int32, (512, 1), 0)
    freq_y = at >> 4
    freq_y = jnp.where(freq_y < GRID // 4, freq_y, freq_y - GRID // 2)
    freq_z = narrow * 8 + ((at & 15) >> 1)
    squared = (freq_x * freq_x + freq_y * freq_y + freq_z * freq_z).astype(F32)
    quarter = float(GRID // 4)
    return 1.0 / jnp.sqrt(1.0 + squared * (1.0 / (quarter * quarter)))


def tile(start, size, unit=16):
    return pl.ds(pl.multiple_of(start, unit), size)


def weigh(w, weights_ref, proj_ref, blocks):
    column = pltpu.roll(weights_ref[0], (128 - w) % 128, 1)[:, 0:1]
    return jnp.concatenate(
        [(proj_ref[block, 0:1024].astype(F32) * column).astype(BF16) for block in blocks], 1
    )


def main_kernel(
    occ_at, emp_at, occ_hbm, emp_hbm, z_first_hbm, z_second_hbm, y_cos_hbm, y_sin_hbm, x_table_hbm, perm_hbm, perm_t_hbm,
    level_hbm, denom_hbm, trial_hbm,
    turned_ref, weights_ref, out_ref, coulomb_ref, early_hbm, early, early_sem,
    occ_ref, emp_ref, z_first, z_second, y_cos, y_sin, x_table, perm_ref, perm_t_ref, level_ref, denom_ref, trial_ref,
    load_sem, x_scr, w_scr, blocks, gathered, columns_f32, waves, pairs, scaled, core_send, core_recv, acc,
    axis_send, axis_recv, z_send, z_recv, z_all,
    narrow_sent, narrow_got, wide_sent, wide_got, send_sem, recv_sem,
):
    wide, narrow = lax.axis_index("wide"), lax.axis_index("narrow")
    x, y, z, core = place()
    x_lo = narrow // 2
    mate = device(x, y, z, 1 - core)
    axis_mates = (
        [device((x + step) % 4, y, z, core) for step in range(1, 4)],
        [device(x, (y + step) % 4, z, core) for step in range(1, 4)],
    )
    z_mates = [device(x, y, (z + step) % 8, core) for step in range(1, 8)]

    loads = [
        pltpu.make_async_copy(src, dst, load_sem.at[at])
        for at, (src, dst) in enumerate(
            (
                (occ_hbm, occ_ref), (emp_hbm, emp_ref), (z_first_hbm, z_first), (z_second_hbm, z_second),
                (y_cos_hbm, y_cos), (y_sin_hbm, y_sin), (x_table_hbm, x_table), (perm_hbm, perm_ref),
                (perm_t_hbm, perm_t_ref), (level_hbm, level_ref), (denom_hbm, denom_ref), (trial_hbm, trial_ref),
            )
        )
    ]
    for copy in loads:
        copy.start()

    barrier = pltpu.get_barrier_semaphore()

    @pl.loop(1, 64)
    def _(step):
        pl.semaphore_signal(barrier, inc=1, device_id=((wide + step) % 64, narrow), device_id_type=MESH)

    for step in range(1, 4):
        pl.semaphore_signal(barrier, inc=1, device_id=(wide, (narrow + step) % 4), device_id_type=MESH)
    across = device(jnp.where(x_lo == 0, (x + 3) % 4, (x + 1) % 4), y, z, core)
    pl.semaphore_signal(barrier, inc=1, device_id=across, device_id_type=MESH)

    def products(half):
        @pl.loop(half * 16, half * 16 + 16)
        def _(pair):
            product = occ_ref[occ_at[pair]] * emp_ref[emp_at[pair]]
            low, high = product[:, :2048], product[:, 2048:]
            rows = tile(pair * 16, 16)
            x_scr[0, rows, :] = low + high
            x_scr[1, rows, :] = low - high

    def narrow_copy(k, half, parity):
        peer = (x_lo + 1 - k // 2) % 2 * 2 + (core + (k + 1) // 2 % 2) % 2
        at = (half * 2 + parity) * 3 + k
        return pltpu.make_async_remote_copy(
            src_ref=blocks.at[k, half, parity], dst_ref=gathered.at[narrow, half, parity],
            send_sem=narrow_sent.at[at], recv_sem=narrow_got.at[at],
            device_id=(wide, peer), device_id_type=MESH,
        )

    def make_table(parity, n):
        first = z_first[n]
        second = z_second[n]

        @pl.loop(0, 2)
        def _(group):
            cos8 = y_cos[parity, tile(group * 16, 16), :]
            sin8 = y_sin[parity, tile(group * 16, 16), :]
            for inner in range(16):
                w_scr[parity * 4 + n, tile(group * 1024 + inner * 64, 64), :] = (
                    first * cos8[inner : inner + 1] + second * sin8[inner : inner + 1]
                )

    def planes(half, parity):
        @pl.loop(0, 4)
        def _(k):
            peer = (x_lo + 1 - k // 2) % 2 * 2 + (core + (k + 1) // 2 % 2) % 2
            if half == 0:
                make_table(parity, peer)
            plane = jnp.dot(
                x_scr[parity, half * 256 : half * 256 + 256], w_scr[parity * 4 + peer], preferred_element_type=F32
            ).astype(BF16)

            @pl.when(k < 3)
            def _():
                blocks[k, half, parity] = plane
                narrow_copy(k, half, parity).start()

            @pl.when(k == 3)
            def _():
                gathered[narrow, half, parity] = plane

    def wide_copy(chunk, peer):
        return pltpu.make_async_remote_copy(
            src_ref=waves.at[chunk, peer], dst_ref=pairs.at[chunk, wide],
            send_sem=wide_sent.at[chunk], recv_sem=wide_got.at[chunk],
            device_id=(peer, narrow), device_id_type=MESH,
        )

    def wide_all(chunk):
        whole = pairs.at[chunk, pl.ds(0, 63)]
        return pltpu.make_async_remote_copy(
            src_ref=whole, dst_ref=whole, send_sem=wide_sent.at[chunk], recv_sem=wide_got.at[chunk],
            device_id=mate, device_id_type=MESH,
        )

    def along_x(chunk):
        half, parity = chunk // 2, chunk % 2
        for k in range(3):
            narrow_copy(k, half, parity).wait_recv()

        @pl.loop(0, 4)
        def _(group):
            stacked = jnp.concatenate(
                [
                    jnp.concatenate(
                        [
                            gathered[n, half, parity, tile(group * 64 + q * 16, 16), part * 128 : part * 128 + 128]
                            for q in range(4)
                        ],
                        1,
                    )
                    for part in range(2)
                    for n in range(4)
                ],
                0,
            )
            result = jnp.dot(x_table[...], stacked, preferred_element_type=F32)
            for q in range(4):
                for part in range(2):
                    columns_f32[part, pl.ds(group * 4 + q, 64, stride=16), :] = result[
                        part * 64 : part * 64 + 64, q * 128 : q * 128 + 128
                    ]

        @pl.loop(0, 8)
        def _(group):
            for part in range(2):
                waves[chunk, tile(group * 8, 8, 8), :, part * 128 : part * 128 + 128] = (
                    columns_f32[part, tile(group * 128, 128), :].astype(BF16).reshape(8, 16, 128)
                )

        @pl.loop(1, 64, unroll=7)
        def _(step):
            wide_copy(chunk, jnp.bitwise_and(wide + step, 63)).start()

        pairs[chunk, wide] = waves[chunk, wide]

    for copy in loads[:7]:
        copy.wait()
    products(0)
    pl.semaphore_wait(barrier, 67)
    planes(0, 0)
    planes(0, 1)
    products(1)
    along_x(0)
    planes(1, 0)
    planes(1, 1)
    for chunk in range(1, 4):
        along_x(chunk)

    for copy in loads[7:]:
        copy.wait()
    column = coulomb_column()
    coulomb_ref[...] = jnp.broadcast_to(column, (512, 128))
    trial = (column * trial_ref[...].astype(F32)).astype(BF16)
    trial = jnp.dot(perm_t_ref[...], trial, preferred_element_type=F32).astype(BF16)
    scaled[0] = jnp.where(core == 0, trial[:, :256], trial[:, 256:])
    scaled[1] = jnp.where(core == 0, trial[:, 256:], trial[:, :256])

    table = denom_ref[...]
    lanes = lax.broadcasted_iota(jnp.int32, (8, 128), 1)
    spread = (lax.broadcasted_iota(jnp.int32, (8, 128), 0) == lanes).astype(F32).astype(BF16)
    onehot = (lax.broadcasted_iota(jnp.int32, (NTAB, 2048), 0) == level_ref[...].reshape(1, 2048)).astype(F32).astype(BF16)
    picked = jnp.zeros((2048, 128), F32)
    for _ in range(3):
        piece = table.astype(BF16)
        table = table - piece.astype(F32)
        piece = lax.dot_general(
            piece, spread, (((0,), (0,)), ((), ())), preferred_element_type=F32
        ).astype(BF16)
        picked += lax.dot_general(onehot, piece, (((0,), (0,)), ((), ())), preferred_element_type=F32)
    picked = picked.reshape(64, 2, 16, 128)
    for half in range(2):
        weights_ref[half] = picked[:, half].reshape(1024, 128)

    count = [0]
    sent = []

    def send(src, dst, peer):
        at = count[0]
        count[0] += 1
        copy = pltpu.make_async_remote_copy(
            src_ref=src, dst_ref=dst, send_sem=send_sem.at[at], recv_sem=recv_sem.at[at],
            device_id=peer, device_id_type=MESH,
        )
        copy.start()
        sent.append(copy)
        return copy

    def project(half, which, rows):
        return jnp.dot(
            pairs[half * 2, pl.ds(rows, 16)].reshape(256, 256), scaled[which, 0:256],
            preferred_element_type=F32,
        ) + jnp.dot(
            pairs[half * 2 + 1, pl.ds(rows, 16)].reshape(256, 256), scaled[which, 256:512],
            preferred_element_type=F32,
        )

    def turn(half):
        @pl.loop(0, 2)
        def _(piece):
            total = jnp.zeros((512, 512), F32)
            for parity in range(2):
                total += lax.dot_general(
                    perm_ref[:, parity * 256 : parity * 256 + 256],
                    pairs[half * 2 + parity, tile(piece * 32, 32)].reshape(512, 256),
                    (((1,), (1,)), ((), ())),
                    preferred_element_type=F32,
                )
            turned_ref[half, :, tile(piece * 512, 512, 512)] = total.astype(BF16)

    def reduce(half):
        for parity in range(2):
            wide_all(half * 2 + parity).wait_recv()
        copies = []
        for piece in range(4):
            rows = pl.ds(piece * 256, 256)
            core_send[half, rows, :] = project(half, 1, piece * 16).astype(BF16)
            copies.append(send(core_send.at[half, rows], core_recv.at[half, rows], mate))
        for piece in range(4):
            own = project(half, 0, piece * 16)
            acc[half, 0, piece * 256 : piece * 256 + 256, :] = own[:, :128]
            acc[half, 1, piece * 256 : piece * 256 + 256, :] = own[:, 128:]
        yield
        for piece in range(4):
            rows = pl.ds(piece * 256, 256)
            copies[piece].wait_recv()
            for h in range(2):
                acc[half, h, rows, :] += core_recv[half, rows, h * 128 : h * 128 + 128].astype(F32)
        base = [0, 0]
        places = ((x, y), (y, x))
        for stage in range(2):
            size = 256 if stage == 0 else 64
            copies = {}
            for h in range(2):
                for step in range(1, 4):
                    rows = tile(base[h] + (places[stage][h] + step) % 4 * size, size)
                    axis_send[half, stage, h, step, 0:size] = acc[half, h, rows, :].astype(BF16)
                    copies[h, step] = send(
                        axis_send.at[half, stage, h, step, pl.ds(0, size)],
                        axis_recv.at[half, stage, h, step, pl.ds(0, size)],
                        axis_mates[(h + stage) % 2][step - 1],
                    )
            yield
            for h in range(2):
                for step in range(1, 4):
                    copies[h, step].wait_recv()
                base[h] = base[h] + places[stage][h] * size
                rows = tile(base[h], size)
                total = acc[half, h, rows, :]
                for step in range(1, 4):
                    total += axis_recv[half, stage, h, step, 0:size].astype(F32)
                acc[half, h, rows, :] = total
        copies = []
        for step in range(1, 8):
            for h in range(2):
                z_send[half, step, h] = acc[half, h, tile(base[h] + (z + step) % 8 * 8, 8, 8), :]
            copies.append(send(z_send.at[half, step], z_recv.at[half, step], z_mates[step - 1]))
        yield
        for copy in copies:
            copy.wait_recv()
        for h in range(2):
            total = acc[half, h, tile(base[h] + z * 8, 8, 8), :]
            for step in range(1, 8):
                total += z_recv[half, step, h]
            z_all[half, z, h] = total
        mine = z_all.at[half, z]
        copies = [send(mine, mine, peer) for peer in z_mates]
        yield
        for copy in copies:
            copy.wait_recv()
        for h in range(2):
            out_ref[core * 2 + h, tile(half * 1024 + base[h], 64), :] = (
                z_all[half, :, h].reshape(64, 128).astype(BF16)
            )
        for stage in (1, 0):
            size = 256 if stage == 0 else 64
            copies = {}
            for h in range(2):
                mine = out_ref.at[core * 2 + h, tile(half * 1024 + base[h], size)]
                for step in range(1, 4):
                    copies[h, step] = send(mine, mine, axis_mates[(h + stage) % 2][step - 1])
            last = []
            if stage == 0:
                for h in range(2):
                    mine = out_ref.at[core * 2 + h, tile(half * 1024 + base[h], size)]
                    last.append(send(mine, mine, mate))
            yield
            for step in range(1, 4):
                for h in range(2):
                    copies[h, step].wait_recv()
                    if stage == 0:
                        start = half * 1024 + (places[0][h] + 4 - step) % 4 * 256
                        piece = out_ref.at[core * 2 + h, tile(start, 256)]
                        last.append(send(piece, piece, mate))
            for h in range(2):
                base[h] = base[h] - places[stage][h] * size
        yield
        for copy in last:
            copy.wait_recv()

    runs = [reduce(half) for half in range(2)]
    def response_copy(w):
        return pltpu.make_async_copy(early.at[w], early_hbm.at[w], early_sem.at[w])

    def respond_early(first, last):
        @pl.loop(first, last)
        def _(w):
            weighted = weigh(w, weights_ref, out_ref, range(4))
            early[w] = jnp.dot(turned_ref[0], weighted, preferred_element_type=F32).astype(BF16)
            response_copy(w).start()

    next(runs[0])
    turn(0)
    for _ in range(3):
        next(runs[0])
    next(runs[1])
    for at in range(4):
        next(runs[0])
        next(runs[1])
        if at == 1:
            turn(1)
    for _ in runs[0]:
        pass
    respond_early(0, 3)
    next(runs[1])
    respond_early(3, 5)
    next(runs[1])
    respond_early(5, 8)
    for _ in runs[1]:
        pass
    for w in range(8):
        response_copy(w).wait()

    for parity in range(2):
        for half in range(2):
            for k in range(3):
                narrow_copy(k, half, parity).wait_send()
    for chunk in range(4):
        wide_all(chunk).wait_send()
    for copy in sent:
        copy.wait_send()


NTAB = 64


def main(pair_occ, pair_emp, *arrays):
    smem = pl.BlockSpec(memory_space=pltpu.SMEM)
    vmem = pl.BlockSpec(memory_space=pltpu.VMEM)
    hbm = pl.BlockSpec(memory_space=pl.ANY)
    copies = 2 * (4 + 12 + 7 + 7 + 12 + 8)
    dma = pltpu.SemaphoreType.DMA
    return pl.pallas_call(
        main_kernel,
        out_shape=(
            jax.ShapeDtypeStruct((2, 512, 1024), BF16),
            jax.ShapeDtypeStruct((2, 1024, 128), F32),
            jax.ShapeDtypeStruct((4, 2048, 128), BF16),
            jax.ShapeDtypeStruct((512, 128), F32),
            jax.ShapeDtypeStruct((8, 512, 512), BF16),
        ),
        in_specs=[smem, smem] + [hbm] * 12,
        out_specs=(vmem, vmem, vmem, vmem, hbm),
        scratch_shapes=[
            pltpu.VMEM((8, 512, 512), BF16),
            dma((8,)),
            *[pltpu.VMEM(array.shape, array.dtype) for array in arrays],
            dma((12,)),
            pltpu.VMEM((2, 512, 2048), BF16),
            pltpu.VMEM((8, 2048, 256), BF16),
            pltpu.VMEM((3, 2, 2, 256, 256), BF16),
            pltpu.VMEM((4, 2, 2, 256, 256), BF16),
            pltpu.VMEM((2, 1024, 128), F32),
            pltpu.VMEM((4, 64, 16, 256), BF16),
            pltpu.VMEM((4, 64, 16, 256), BF16),
            pltpu.VMEM((2, 512, 256), BF16),
            pltpu.VMEM((2, 1024, 256), BF16),
            pltpu.VMEM((2, 1024, 256), BF16),
            pltpu.VMEM((2, 2, 1024, 128), F32),
            pltpu.VMEM((2, 2, 2, 4, 256, 128), BF16),
            pltpu.VMEM((2, 2, 2, 4, 256, 128), BF16),
            pltpu.VMEM((2, 8, 2, 8, 128), F32),
            pltpu.VMEM((2, 8, 2, 8, 128), F32),
            pltpu.VMEM((2, 8, 2, 8, 128), F32),
            dma((12,)), dma((12,)), dma((4,)), dma((4,)), dma((copies,)), dma((copies,)),
        ],
        compiler_params=pltpu.CompilerParams(vmem_limit_bytes=MAIN_LIMIT, collective_id=0, has_side_effects=True),
        name="main",
    )(pair_occ, pair_emp, *arrays)


def response_kernel(early_ref, turned_ref, weights_ref, proj_ref, coulomb_ref, out_ref, even, odd):
    step = pl.program_id(0)

    @pl.when(step == 0)
    def _():
        even[...] = weigh(0, weights_ref, proj_ref, range(4))

    column = jnp.concatenate([coulomb_ref[...]] * 2, 1)
    for at, (now, later) in enumerate(((even, odd), (odd, even))):
        for lanes in range(2):
            span = slice(lanes * 256, lanes * 256 + 256)
            total = jnp.dot(turned_ref[0], now[:, span], preferred_element_type=F32)
            later[:, span] = weigh(step * 2 + at + 1, weights_ref, proj_ref, range(lanes * 2, lanes * 2 + 2))
            out_ref[at, :, span] = ((early_ref[at, :, span].astype(F32) + total) * column).astype(BF16)


def respond(early, turned, weights, projections, coulomb):
    return pl.pallas_call(
        response_kernel,
        out_shape=jax.ShapeDtypeStruct((8, 512, 512), BF16),
        grid=(4,),
        in_specs=[
            pl.BlockSpec((2, 512, 512), lambda w: (w, 0, 0)),
            pl.BlockSpec((1, 512, 1024), lambda w: (1, 0, 0)),
            pl.BlockSpec((1, 1024, 128), lambda w: (1, 0, 0)),
            pl.BlockSpec((4, 1024, 128), lambda w: (0, 1, 0)),
            pl.BlockSpec((512, 128), lambda w: (0, 0)),
        ],
        out_specs=pl.BlockSpec((2, 512, 512), lambda w: (w, 0, 0)),
        scratch_shapes=[pltpu.VMEM((1024, 512), BF16), pltpu.VMEM((1024, 512), BF16)],
        compiler_params=pltpu.CompilerParams(vmem_limit_bytes=RESPOND_LIMIT),
        name="respond",
    )(early, turned, weights, projections, coulomb)


def shards(occupied, empty, pair_occ, pair_emp, pair_level, denominators, trial):
    constants = [jnp.asarray(t) for t in tables()]
    turned, weights, projections, coulomb, early = main(
        pair_occ, pair_emp, occupied, empty, *constants,
        pair_level, denominators.T, trial,
    )
    return respond(early, turned, weights, projections, coulomb)


def solution(mesh):
    placed = (
        P("wide", "narrow", None),
        P("wide", "narrow", None),
        P("wide"),
        P("wide"),
        P(),
        P(),
        P(("wide", "narrow"), None),
    )
    return jax.shard_map(
        shards,
        mesh=mesh,
        in_specs=placed,
        out_specs=P(None, ("wide", "narrow"), None),
        check_vma=False,
    )
```

```python
import math

import jax
import jax.numpy as jnp
import ml_dtypes
import numpy as np
from jax import lax
from jax.experimental import pallas as pl
from jax.experimental.pallas import tpu as pltpu
from jax.sharding import PartitionSpec as P

GRID = 64
MESH = pl.DeviceIdType.MESH
F32, BF16 = jnp.float32, jnp.bfloat16
MAIN_LIMIT = 62 * 1024 * 1024
RESPOND_LIMIT = 60 * 1024 * 1024


def rounded(values):
    return values.astype(np.float32).astype(ml_dtypes.bfloat16).astype(np.float32)


def tables():
    at = np.arange(GRID)
    half = np.arange(GRID // 2)
    scaling = 1.0 / math.sqrt(GRID)
    step = 2.0 * math.pi / GRID
    z_angles = (at[:, None] * half[None, :] % GRID) * step
    z_real = rounded(scaling * np.cos(z_angles))
    z_imag = rounded(-scaling * np.sin(z_angles))
    signed = np.where(half < GRID // 4, half, half - GRID // 2)
    y_angles = (signed[:, None] * at[None, :] % GRID) * step
    y_cos = rounded(scaling * np.cos(y_angles))
    y_sin = rounded(scaling * np.sin(y_angles))
    x_angles = (at[:, None] * at[None, :] % GRID) * step
    x_cos = rounded(scaling * np.cos(x_angles))
    x_sin = rounded(scaling * np.sin(x_angles))
    zr = z_real.reshape(GRID, 4, 8).transpose(1, 0, 2)
    zi = z_imag.reshape(GRID, 4, 8).transpose(1, 0, 2)

    def spread(first, second):
        both = np.stack([first, second], 2)[:, :, :, None, :]
        return np.broadcast_to(both, (4, GRID, 2, 16, 8)).reshape(4, GRID, 256)

    z_first = spread(zr, zi)
    z_second = spread(zi, -zr)

    def widen(table):
        table = table[:, :32].reshape(16, 2, 32).transpose(1, 2, 0)
        return np.broadcast_to(table[:, :, None, :, None], (2, 32, 2, 16, 8)).reshape(2, 32, 256)

    x_table = np.block([[x_cos, x_sin], [-x_sin, x_cos]])
    perm = np.zeros((512, 512), np.float32)
    parity, part, j16, kz8 = np.meshgrid(np.arange(2), np.arange(2), np.arange(16), np.arange(8), indexing="ij")
    inner = np.arange(512)
    outer = ((2 * j16 + parity) * 16 + 2 * kz8 + part).reshape(-1)
    perm[outer, inner] = 1.0
    small = [z_first, z_second, widen(y_cos), widen(y_sin), x_table, perm, perm.T]
    return [np.ascontiguousarray(t).astype(ml_dtypes.bfloat16) for t in small]


def place():
    wide, narrow = lax.axis_index("wide"), lax.axis_index("narrow")
    z, x_hi, y = wide // 8, wide // 4 % 2, wide % 4
    x_lo, core = narrow // 2, narrow % 2
    return x_hi * 2 + x_lo, y, z, core


def device(x, y, z, core):
    return (z * 8 + x // 2 * 4 + y, x % 2 * 2 + core)


def coulomb_column():
    freq_x, narrow = lax.axis_index("wide"), lax.axis_index("narrow")
    freq_x = jnp.where(freq_x < GRID // 2, freq_x, freq_x - GRID)
    at = lax.broadcasted_iota(jnp.int32, (512, 1), 0)
    freq_y = at >> 4
    freq_y = jnp.where(freq_y < GRID // 4, freq_y, freq_y - GRID // 2)
    freq_z = narrow * 8 + ((at & 15) >> 1)
    squared = (freq_x * freq_x + freq_y * freq_y + freq_z * freq_z).astype(F32)
    quarter = float(GRID // 4)
    return 1.0 / jnp.sqrt(1.0 + squared * (1.0 / (quarter * quarter)))


def tile(start, size, unit=16):
    return pl.ds(pl.multiple_of(start, unit), size)


def weigh(w, weights_ref, proj_ref, blocks):
    column = pltpu.roll(weights_ref[0], (128 - w) % 128, 1)[:, 0:1]
    return jnp.concatenate(
        [(proj_ref[block, 0:1024].astype(F32) * column).astype(BF16) for block in blocks], 1
    )


def main_kernel(
    occ_at, emp_at, occ_hbm, emp_hbm, z_first_hbm, z_second_hbm, y_cos_hbm, y_sin_hbm, x_table_hbm, perm_hbm, perm_t_hbm,
    level_hbm, denom_hbm, trial_hbm,
    turned_ref, weights_ref, out_ref, coulomb_ref, early_hbm, early, early_sem,
    occ_ref, emp_ref, z_first, z_second, y_cos, y_sin, x_table, perm_ref, perm_t_ref, level_ref, denom_ref, trial_ref,
    load_sem, x_scr, w_scr, blocks, gathered, columns_f32, waves, pairs, scaled, core_send, core_recv, acc,
    axis_send, axis_recv, z_send, z_recv, z_all,
    narrow_sent, narrow_got, wide_sent, wide_got, send_sem, recv_sem,
):
    wide, narrow = lax.axis_index("wide"), lax.axis_index("narrow")
    x, y, z, core = place()
    x_lo = narrow // 2
    mate = device(x, y, z, 1 - core)
    axis_mates = (
        [device((x + step) % 4, y, z, core) for step in range(1, 4)],
        [device(x, (y + step) % 4, z, core) for step in range(1, 4)],
    )
    z_mates = [device(x, y, (z + step) % 8, core) for step in range(1, 8)]

    loads = [
        pltpu.make_async_copy(src, dst, load_sem.at[at])
        for at, (src, dst) in enumerate(
            (
                (occ_hbm, occ_ref), (emp_hbm, emp_ref), (z_first_hbm, z_first), (z_second_hbm, z_second),
                (y_cos_hbm, y_cos), (y_sin_hbm, y_sin), (x_table_hbm, x_table), (perm_hbm, perm_ref),
                (perm_t_hbm, perm_t_ref), (level_hbm, level_ref), (denom_hbm, denom_ref), (trial_hbm, trial_ref),
            )
        )
    ]
    for copy in loads:
        copy.start()

    barrier = pltpu.get_barrier_semaphore()

    @pl.loop(1, 64)
    def _(step):
        pl.semaphore_signal(barrier, inc=1, device_id=((wide + step) % 64, narrow), device_id_type=MESH)

    for step in range(1, 4):
        pl.semaphore_signal(barrier, inc=1, device_id=(wide, (narrow + step) % 4), device_id_type=MESH)
    across = device(jnp.where(x_lo == 0, (x + 3) % 4, (x + 1) % 4), y, z, core)
    pl.semaphore_signal(barrier, inc=1, device_id=across, device_id_type=MESH)

    def products(half):
        @pl.loop(half * 16, half * 16 + 16)
        def _(pair):
            product = occ_ref[occ_at[pair]] * emp_ref[emp_at[pair]]
            low, high = product[:, :2048], product[:, 2048:]
            rows = tile(pair * 16, 16)
            x_scr[0, rows, :] = low + high
            x_scr[1, rows, :] = low - high

    def narrow_copy(k, half, parity):
        peer = (x_lo + 1 - k // 2) % 2 * 2 + (core + (k + 1) // 2 % 2) % 2
        at = (half * 2 + parity) * 3 + k
        return pltpu.make_async_remote_copy(
            src_ref=blocks.at[k, half, parity], dst_ref=gathered.at[narrow, half, parity],
            send_sem=narrow_sent.at[at], recv_sem=narrow_got.at[at],
            device_id=(wide, peer), device_id_type=MESH,
        )

    def make_table(parity, n):
        first = z_first[n]
        second = z_second[n]

        @pl.loop(0, 2)
        def _(group):
            cos8 = y_cos[parity, tile(group * 16, 16), :]
            sin8 = y_sin[parity, tile(group * 16, 16), :]
            for inner in range(16):
                w_scr[parity * 4 + n, tile(group * 1024 + inner * 64, 64), :] = (
                    first * cos8[inner : inner + 1] + second * sin8[inner : inner + 1]
                )

    def planes(half, parity):
        @pl.loop(0, 4)
        def _(k):
            peer = (x_lo + 1 - k // 2) % 2 * 2 + (core + (k + 1) // 2 % 2) % 2
            if half == 0:
                make_table(parity, peer)
            plane = jnp.dot(
                x_scr[parity, half * 256 : half * 256 + 256], w_scr[parity * 4 + peer], preferred_element_type=F32
            ).astype(BF16)

            @pl.when(k < 3)
            def _():
                blocks[k, half, parity] = plane
                narrow_copy(k, half, parity).start()

            @pl.when(k == 3)
            def _():
                gathered[narrow, half, parity] = plane

    def wide_copy(chunk, peer):
        return pltpu.make_async_remote_copy(
            src_ref=waves.at[chunk, peer], dst_ref=pairs.at[chunk, wide],
            send_sem=wide_sent.at[chunk], recv_sem=wide_got.at[chunk],
            device_id=(peer, narrow), device_id_type=MESH,
        )

    def wide_all(chunk):
        whole = pairs.at[chunk, pl.ds(0, 63)]
        return pltpu.make_async_remote_copy(
            src_ref=whole, dst_ref=whole, send_sem=wide_sent.at[chunk], recv_sem=wide_got.at[chunk],
            device_id=mate, device_id_type=MESH,
        )

    def along_x(chunk):
        half, parity = chunk // 2, chunk % 2
        for k in range(3):
            narrow_copy(k, half, parity).wait_recv()

        @pl.loop(0, 4)
        def _(group):
            stacked = jnp.concatenate(
                [
                    jnp.concatenate(
                        [
                            gathered[n, half, parity, tile(group * 64 + q * 16, 16), part * 128 : part * 128 + 128]
                            for q in range(4)
                        ],
                        1,
                    )
                    for part in range(2)
                    for n in range(4)
                ],
                0,
            )
            result = jnp.dot(x_table[...], stacked, preferred_element_type=F32)
            for q in range(4):
                for part in range(2):
                    columns_f32[part, pl.ds(group * 4 + q, 64, stride=16), :] = result[
                        part * 64 : part * 64 + 64, q * 128 : q * 128 + 128
                    ]

        @pl.loop(0, 8)
        def _(group):
            for part in range(2):
                waves[chunk, tile(group * 8, 8, 8), :, part * 128 : part * 128 + 128] = (
                    columns_f32[part, tile(group * 128, 128), :].astype(BF16).reshape(8, 16, 128)
                )

        @pl.loop(1, 64, unroll=7)
        def _(step):
            wide_copy(chunk, jnp.bitwise_and(wide + step, 63)).start()

        pairs[chunk, wide] = waves[chunk, wide]

    for copy in loads[:7]:
        copy.wait()
    products(0)
    pl.semaphore_wait(barrier, 67)
    planes(0, 0)
    planes(0, 1)
    products(1)
    along_x(0)
    planes(1, 0)
    planes(1, 1)
    for chunk in range(1, 4):
        along_x(chunk)

    for copy in loads[7:]:
        copy.wait()
    column = coulomb_column()
    coulomb_ref[...] = jnp.broadcast_to(column, (512, 128))
    trial = (column * trial_ref[...].astype(F32)).astype(BF16)
    trial = jnp.dot(perm_t_ref[...], trial, preferred_element_type=F32).astype(BF16)
    scaled[0] = jnp.where(core == 0, trial[:, :256], trial[:, 256:])
    scaled[1] = jnp.where(core == 0, trial[:, 256:], trial[:, :256])

    table = denom_ref[...]
    lanes = lax.broadcasted_iota(jnp.int32, (8, 128), 1)
    spread = (lax.broadcasted_iota(jnp.int32, (8, 128), 0) == lanes).astype(F32).astype(BF16)
    onehot = (lax.broadcasted_iota(jnp.int32, (NTAB, 2048), 0) == level_ref[...].reshape(1, 2048)).astype(F32).astype(BF16)
    picked = jnp.zeros((2048, 128), F32)
    for _ in range(3):
        piece = table.astype(BF16)
        table = table - piece.astype(F32)
        piece = lax.dot_general(
            piece, spread, (((0,), (0,)), ((), ())), preferred_element_type=F32
        ).astype(BF16)
        picked += lax.dot_general(onehot, piece, (((0,), (0,)), ((), ())), preferred_element_type=F32)
    picked = picked.reshape(64, 2, 16, 128)
    for half in range(2):
        weights_ref[half] = picked[:, half].reshape(1024, 128)

    count = [0]
    sent = []

    def send(src, dst, peer):
        at = count[0]
        count[0] += 1
        copy = pltpu.make_async_remote_copy(
            src_ref=src, dst_ref=dst, send_sem=send_sem.at[at], recv_sem=recv_sem.at[at],
            device_id=peer, device_id_type=MESH,
        )
        copy.start()
        sent.append(copy)
        return copy

    def project(half, which, rows):
        return jnp.dot(
            pairs[half * 2, pl.ds(rows, 16)].reshape(256, 256), scaled[which, 0:256],
            preferred_element_type=F32,
        ) + jnp.dot(
            pairs[half * 2 + 1, pl.ds(rows, 16)].reshape(256, 256), scaled[which, 256:512],
            preferred_element_type=F32,
        )

    def turn(half):
        @pl.loop(0, 2)
        def _(piece):
            total = jnp.zeros((512, 512), F32)
            for parity in range(2):
                total += lax.dot_general(
                    perm_ref[:, parity * 256 : parity * 256 + 256],
                    pairs[half * 2 + parity, tile(piece * 32, 32)].reshape(512, 256),
                    (((1,), (1,)), ((), ())),
                    preferred_element_type=F32,
                )
            turned_ref[half, :, tile(piece * 512, 512, 512)] = total.astype(BF16)

    def reduce(half):
        for parity in range(2):
            wide_all(half * 2 + parity).wait_recv()
        copies = []
        for piece in range(4):
            rows = pl.ds(piece * 256, 256)
            core_send[half, rows, :] = project(half, 1, piece * 16).astype(BF16)
            copies.append(send(core_send.at[half, rows], core_recv.at[half, rows], mate))
        for piece in range(4):
            own = project(half, 0, piece * 16)
            acc[half, 0, piece * 256 : piece * 256 + 256, :] = own[:, :128]
            acc[half, 1, piece * 256 : piece * 256 + 256, :] = own[:, 128:]
        yield
        for piece in range(4):
            rows = pl.ds(piece * 256, 256)
            copies[piece].wait_recv()
            for h in range(2):
                acc[half, h, rows, :] += core_recv[half, rows, h * 128 : h * 128 + 128].astype(F32)
        base = [0, 0]
        places = ((x, y), (y, x))
        for stage in range(2):
            size = 256 if stage == 0 else 64
            copies = {}
            for h in range(2):
                for step in range(1, 4):
                    rows = tile(base[h] + (places[stage][h] + step) % 4 * size, size)
                    axis_send[half, stage, h, step, 0:size] = acc[half, h, rows, :].astype(BF16)
                    copies[h, step] = send(
                        axis_send.at[half, stage, h, step, pl.ds(0, size)],
                        axis_recv.at[half, stage, h, step, pl.ds(0, size)],
                        axis_mates[(h + stage) % 2][step - 1],
                    )
            yield
            for h in range(2):
                for step in range(1, 4):
                    copies[h, step].wait_recv()
                base[h] = base[h] + places[stage][h] * size
                rows = tile(base[h], size)
                total = acc[half, h, rows, :]
                for step in range(1, 4):
                    total += axis_recv[half, stage, h, step, 0:size].astype(F32)
                acc[half, h, rows, :] = total
        copies = []
        for step in range(1, 8):
            for h in range(2):
                z_send[half, step, h] = acc[half, h, tile(base[h] + (z + step) % 8 * 8, 8, 8), :]
            copies.append(send(z_send.at[half, step], z_recv.at[half, step], z_mates[step - 1]))
        yield
        for copy in copies:
            copy.wait_recv()
        for h in range(2):
            total = acc[half, h, tile(base[h] + z * 8, 8, 8), :]
            for step in range(1, 8):
                total += z_recv[half, step, h]
            z_all[half, z, h] = total
        mine = z_all.at[half, z]
        copies = [send(mine, mine, peer) for peer in z_mates]
        yield
        for copy in copies:
            copy.wait_recv()
        for h in range(2):
            out_ref[core * 2 + h, tile(half * 1024 + base[h], 64), :] = (
                z_all[half, :, h].reshape(64, 128).astype(BF16)
            )
        for stage in (1, 0):
            size = 256 if stage == 0 else 64
            copies = {}
            for h in range(2):
                mine = out_ref.at[core * 2 + h, tile(half * 1024 + base[h], size)]
                for step in range(1, 4):
                    copies[h, step] = send(mine, mine, axis_mates[(h + stage) % 2][step - 1])
            last = []
            if stage == 0:
                for h in range(2):
                    mine = out_ref.at[core * 2 + h, tile(half * 1024 + base[h], size)]
                    last.append(send(mine, mine, mate))
            yield
            for step in range(1, 4):
                for h in range(2):
                    copies[h, step].wait_recv()
                    if stage == 0:
                        start = half * 1024 + (places[0][h] + 4 - step) % 4 * 256
                        piece = out_ref.at[core * 2 + h, tile(start, 256)]
                        last.append(send(piece, piece, mate))
            for h in range(2):
                base[h] = base[h] - places[stage][h] * size
        yield
        for copy in last:
            copy.wait_recv()

    runs = [reduce(half) for half in range(2)]
    def response_copy(w):
        return pltpu.make_async_copy(early.at[w], early_hbm.at[w], early_sem.at[w])

    def respond_early(first, last):
        @pl.loop(first, last)
        def _(w):
            weighted = weigh(w, weights_ref, out_ref, range(4))
            early[w] = jnp.dot(turned_ref[0], weighted, preferred_element_type=F32).astype(BF16)
            response_copy(w).start()

    next(runs[0])
    turn(0)
    for _ in range(3):
        next(runs[0])
    next(runs[1])
    for at in range(4):
        next(runs[1])
        next(runs[0])
        if at == 1:
            turn(1)
    for _ in runs[0]:
        pass
    respond_early(0, 3)
    next(runs[1])
    respond_early(3, 5)
    next(runs[1])
    respond_early(5, 8)
    for _ in runs[1]:
        pass
    for w in range(8):
        response_copy(w).wait()

    for parity in range(2):
        for half in range(2):
            for k in range(3):
                narrow_copy(k, half, parity).wait_send()
    for chunk in range(4):
        wide_all(chunk).wait_send()
    for copy in sent:
        copy.wait_send()


NTAB = 64


def main(pair_occ, pair_emp, *arrays):
    smem = pl.BlockSpec(memory_space=pltpu.SMEM)
    vmem = pl.BlockSpec(memory_space=pltpu.VMEM)
    hbm = pl.BlockSpec(memory_space=pl.ANY)
    copies = 2 * (4 + 12 + 7 + 7 + 12 + 8)
    dma = pltpu.SemaphoreType.DMA
    return pl.pallas_call(
        main_kernel,
        out_shape=(
            jax.ShapeDtypeStruct((2, 512, 1024), BF16),
            jax.ShapeDtypeStruct((2, 1024, 128), F32),
            jax.ShapeDtypeStruct((4, 2048, 128), BF16),
            jax.ShapeDtypeStruct((512, 128), F32),
            jax.ShapeDtypeStruct((8, 512, 512), BF16),
        ),
        in_specs=[smem, smem] + [hbm] * 12,
        out_specs=(vmem, vmem, vmem, vmem, hbm),
        scratch_shapes=[
            pltpu.VMEM((8, 512, 512), BF16),
            dma((8,)),
            *[pltpu.VMEM(array.shape, array.dtype) for array in arrays],
            dma((12,)),
            pltpu.VMEM((2, 512, 2048), BF16),
            pltpu.VMEM((8, 2048, 256), BF16),
            pltpu.VMEM((3, 2, 2, 256, 256), BF16),
            pltpu.VMEM((4, 2, 2, 256, 256), BF16),
            pltpu.VMEM((2, 1024, 128), F32),
            pltpu.VMEM((4, 64, 16, 256), BF16),
            pltpu.VMEM((4, 64, 16, 256), BF16),
            pltpu.VMEM((2, 512, 256), BF16),
            pltpu.VMEM((2, 1024, 256), BF16),
            pltpu.VMEM((2, 1024, 256), BF16),
            pltpu.VMEM((2, 2, 1024, 128), F32),
            pltpu.VMEM((2, 2, 2, 4, 256, 128), BF16),
            pltpu.VMEM((2, 2, 2, 4, 256, 128), BF16),
            pltpu.VMEM((2, 8, 2, 8, 128), F32),
            pltpu.VMEM((2, 8, 2, 8, 128), F32),
            pltpu.VMEM((2, 8, 2, 8, 128), F32),
            dma((12,)), dma((12,)), dma((4,)), dma((4,)), dma((copies,)), dma((copies,)),
        ],
        compiler_params=pltpu.CompilerParams(vmem_limit_bytes=MAIN_LIMIT, collective_id=0, has_side_effects=True),
        name="main",
    )(pair_occ, pair_emp, *arrays)


def response_kernel(early_ref, turned_ref, weights_ref, proj_ref, coulomb_ref, out_ref, even, odd):
    step = pl.program_id(0)

    @pl.when(step == 0)
    def _():
        even[...] = weigh(0, weights_ref, proj_ref, range(4))

    column = jnp.concatenate([coulomb_ref[...]] * 2, 1)
    for at, (now, later) in enumerate(((even, odd), (odd, even))):
        for lanes in range(2):
            span = slice(lanes * 256, lanes * 256 + 256)
            total = jnp.dot(turned_ref[0], now[:, span], preferred_element_type=F32)
            later[:, span] = weigh(step * 2 + at + 1, weights_ref, proj_ref, range(lanes * 2, lanes * 2 + 2))
            out_ref[at, :, span] = ((early_ref[at, :, span].astype(F32) + total) * column).astype(BF16)


def respond(early, turned, weights, projections, coulomb):
    return pl.pallas_call(
        response_kernel,
        out_shape=jax.ShapeDtypeStruct((8, 512, 512), BF16),
        grid=(4,),
        in_specs=[
            pl.BlockSpec((2, 512, 512), lambda w: (w, 0, 0)),
            pl.BlockSpec((1, 512, 1024), lambda w: (1, 0, 0)),
            pl.BlockSpec((1, 1024, 128), lambda w: (1, 0, 0)),
            pl.BlockSpec((4, 1024, 128), lambda w: (0, 1, 0)),
            pl.BlockSpec((512, 128), lambda w: (0, 0)),
        ],
        out_specs=pl.BlockSpec((2, 512, 512), lambda w: (w, 0, 0)),
        scratch_shapes=[pltpu.VMEM((1024, 512), BF16), pltpu.VMEM((1024, 512), BF16)],
        compiler_params=pltpu.CompilerParams(vmem_limit_bytes=RESPOND_LIMIT),
        name="respond",
    )(early, turned, weights, projections, coulomb)


def shards(occupied, empty, pair_occ, pair_emp, pair_level, denominators, trial):
    constants = [jnp.asarray(t) for t in tables()]
    turned, weights, projections, coulomb, early = main(
        pair_occ, pair_emp, occupied, empty, *constants,
        pair_level, denominators.T, trial,
    )
    return respond(early, turned, weights, projections, coulomb)


def solution(mesh):
    placed = (
        P("wide", "narrow", None),
        P("wide", "narrow", None),
        P("wide"),
        P("wide"),
        P(),
        P(),
        P(("wide", "narrow"), None),
    )
    return jax.shard_map(
        shards,
        mesh=mesh,
        in_specs=placed,
        out_specs=P(None, ("wide", "narrow"), None),
        check_vma=False,
    )
```
